256 devices in a mesh: op: 64 (over y, z_hi, x, core), sec: 4 (over z_lo).
Axes of the slice: x: 4, y: 4, z: 8 (z_hi: 2, z_lo: 4; z = z_hi * 4 + z_lo), core: 2. Of those that a mesh axis runs over, the one named last changes fastest.
Arguments:
- wavefunction: bfloat16 [16, 256, 256], P('sec'), may hold values from -6 to 6
- left_operators: bfloat16 [256, 16, 256, 256], P('op', 'sec'), may hold values from -0.375 to 0.375
- right_operators: bfloat16 [256, 16, 256, 256], P('op', 'sec'), may hold values from -0.375 to 0.375
- rotations: bfloat16 [16, 256, 256], P('sec'), may hold values from -0.375 to 0.375
- charges: int32 [256], P('op'), may hold values from -1 to 1
- present_blocks: int32 [256, 16], P('op', 'sec'), may hold values 0 or 1
- directions: int32 [256, 1], P('op'), may hold values from 0 to 3, as said below
Outputs:
- sigma_vector: float32 [16, 256, 256], P('sec', 'op')
- regrouped: bfloat16 [512, 16, 256, 256], P('op', 'sec')
The draws below stay inside these ranges and needn't reach their ends.
Inputs may be any that keep to these rules, and one draw needn't show every extreme that they name: `directions`: among the pairs of one index of op, each direction is named by at most 2 pairs, some direction is named by exactly 2, and every direction other than 0 is named at least once.
All inputs are finite; a program needn't handle non-finite values. No bound on the sum of `present_blocks` on one device may be relied on, other than what follows from the above.
Results may differ from the reference program's by a relative error of at most 0.0049.
Values may be sent and summed in bfloat16 or wider, within the bound.
A program may use at most 64 MiB of HBM per device.

```python
import math
import jax
import jax.numpy as jnp
from jax import lax

MB = 256
P_DEV = 4
DIRS = 4
CAPS = 2
NSEC = 16
PAIRS = 256
N_OP = 64


def draw_directions(key, part):
    owners = PAIRS // P_DEV
    first_key = jax.random.fold_in(key, 71)
    second_key = jax.random.fold_in(key, 72)
    extra = jax.random.randint(first_key, (owners,), 1, DIRS).astype(jnp.int32)
    base = (jnp.arange(P_DEV, dtype=jnp.int32) % DIRS).astype(jnp.int32)
    column = jnp.arange(P_DEV, dtype=jnp.int32)[None, :]
    layout = jnp.where(column == 0, extra[:, None], base[None, :]).astype(jnp.int32)
    row_keys = jax.random.split(second_key, owners)
    shuffled = jax.vmap(lambda row_key, row: jax.random.permutation(row_key, row))(row_keys, layout)
    return shuffled.reshape(PAIRS, 1).astype(jnp.int32)


def plant(drawn, rng, smallest, largest):
    index_at = [jax.random.randint(jax.random.fold_in(rng, axis), (), 0, length) for axis, length in enumerate(drawn.shape)]
    widest = drawn.shape.index(max(drawn.shape))
    next_to = index_at[:widest] + [(index_at[widest] + 1) % drawn.shape[widest]] + index_at[widest + 1:]
    return drawn.at[tuple(index_at)].set(smallest).at[tuple(next_to)].set(largest)


def level_of(rng, extent, shards, smallest, top_value):
    def one(dim, parts):
        heights = jax.random.uniform(jax.random.fold_in(jax.random.fold_in(rng, 6), dim), (parts,), jnp.float32, smallest / len(shards), top_value / len(shards))
        return jnp.repeat(jnp.exp(heights), extent[dim] // parts).reshape((-1,) + (1,) * (len(extent) - dim - 1))

    factor_of = one(*shards[0])
    for cut in shards[1:]:
        factor_of = factor_of * one(*cut)
    return factor_of


def noise(stream_key, dims, width, reach, cuts=(), kind=jnp.bfloat16):
    result = width * jax.random.normal(stream_key, dims, jnp.float32)
    if cuts:
        result = result * level_of(stream_key, dims, cuts, -0.22, 0.18)
    return jnp.clip(result, -reach, reach).astype(kind)


def setup_inputs(seed: int = 0) -> dict:
    keys = jax.random.split(jax.random.key(seed), 8)
    return {
        "wavefunction": noise(keys[0], (NSEC, MB, MB), 1.0, 6.0, ((0, 4),)),
        "left_operators": noise(keys[1], (PAIRS, NSEC, MB, MB), MB ** -0.5, 0.375, ((0, 64), (1, 4))),
        "right_operators": noise(keys[2], (PAIRS, NSEC, MB, MB), MB ** -0.5, 0.375, ((0, 64), (1, 4))),
        "rotations": noise(keys[3], (NSEC, MB, MB), MB ** -0.5, 0.375, ((0, 4),)),
        "charges": plant(jax.random.randint(keys[4], (PAIRS,), -1, 2), jax.random.fold_in(keys[4], 1), -1, 1).astype(jnp.int32),
        "present_blocks": plant((jax.random.randint(keys[5], (PAIRS, NSEC), 0, 4) < 3).astype(jnp.int32), jax.random.fold_in(keys[5], 1), 0, 1),
        "directions": draw_directions(jax.random.fold_in(keys[7], 71), 0),
    }


def reference(wavefunction, left_operators, right_operators, rotations, charges, present_blocks, directions):
    psi_full = wavefunction.astype(jnp.float32)
    rot_full = rotations.astype(jnp.float32)
    rot_padded = jnp.pad(rot_full, ((1, 1), (0, 0), (0, 0)))
    sectors = jnp.arange(NSEC, dtype=jnp.int32)

    def per_pair(carry, inputs):
        left, right, charge, present = inputs
        weight = present.astype(jnp.float32)[:, None, None]
        halfway = jnp.einsum('sij,sjk->sik', left.astype(jnp.float32), psi_full).astype(jnp.bfloat16)
        products = jnp.einsum('sik,smk->sim', halfway.astype(jnp.float32), right.astype(jnp.float32)) * weight
        indices = (sectors + 1 + charge).astype(jnp.int32)
        carry = carry.at[indices].add(products)
        rotated = jnp.einsum('sij,sjk->sik', left.astype(jnp.float32), rot_full).astype(jnp.bfloat16)
        target = rot_padded[indices]
        renormed = (jnp.einsum('sji,sjk->sik', target, rotated.astype(jnp.float32)) * weight).astype(jnp.bfloat16)
        return (carry, renormed)
    start = jnp.zeros((NSEC + 2, MB, MB), jnp.float32)
    extended, renormed = lax.scan(per_pair, start, (left_operators, right_operators, charges, present_blocks))
    sigma_vector = extended[1:NSEC + 1] / math.sqrt(PAIRS)
    kinds = directions[:, 0].reshape(N_OP, P_DEV)
    matching = kinds[:, :, None] == kinds[:, None, :]
    earlier = jnp.arange(P_DEV)[None, :] < jnp.arange(P_DEV)[:, None]
    position = lax.optimization_barrier(jnp.sum(jnp.logical_and(matching, earlier[None]), axis=2)).astype(jnp.int32).reshape(PAIRS)
    offsets = jnp.array([0, 1, -1, N_OP // 2], dtype=jnp.int32)
    kind_flat = directions[:, 0].astype(jnp.int32)
    device = (jnp.arange(PAIRS, dtype=jnp.int32) // P_DEV).astype(jnp.int32)
    destination = (device + offsets[kind_flat]) % N_OP
    slot_index = (destination * DIRS * CAPS + kind_flat * CAPS + position).astype(jnp.int32)
    regrouped = jnp.zeros((N_OP * DIRS * CAPS, NSEC, MB, MB), jnp.bfloat16).at[slot_index].set(renormed)
    return (sigma_vector, regrouped)
```

```python
import jax
import jax.numpy as jnp
from jax import lax
from jax.experimental import pallas as pl
from jax.experimental.pallas import tpu as pltpu
from jax.sharding import PartitionSpec as P

MESH = pl.DeviceIdType.MESH
F32 = jnp.float32
BF16 = jnp.bfloat16
NT = (((1,), (1,)), ((), ()))


def place(y, zh, x, c):
    return y * 16 + zh * 8 + x * 2 + c


def kernel(
    chg, pres, dirs, psi_h, left_h, right_h, rot_h,
    sig, reg,
    psi, left, right, rot, rot_t, rot_in, half, rotd, pay, zero_blk,
    part, c_in, x_out, x_in, f2, y_out, y_in, z_out, z_in, e_out, e_in,
    in_sem, rot_s, rot_r, pay_s, pay_r, loc_sem, c_s, c_r, x_s, x_r, y_s, y_r, z_s, z_r, e_s, e_r,
):
    d = lax.axis_index("op")
    s = lax.axis_index("sec")
    y, zh, x, c = d // 16, (d // 8) % 2, (d // 2) % 4, d % 2
    core_peer = place(y, zh, x, 1 - c)
    x_peer = [place(y, zh, (x + o) % 4, c) for o in (1, 2, 3)]
    y_peer = [place((y + o) % 4, zh, x, c) for o in (1, 2, 3)]
    zh_peer = place(y, 1 - zh, x, c)
    up, down, across = (d + 1) % 64, (d + 63) % 64, (d + 32) % 64

    loads = [
        pltpu.make_async_copy(rot_h, rot, in_sem.at[0]),
        pltpu.make_async_copy(psi_h, psi, in_sem.at[1]),
    ]
    for p in range(4):
        loads.append(pltpu.make_async_copy(left_h.at[pl.ds(4 * p, 4)], left.at[pl.ds(4 * p, 4)], in_sem.at[2 + p]))
    loads.append(pltpu.make_async_copy(right_h, right, in_sem.at[6]))

    bar = pltpu.get_barrier_semaphore()
    for peer in [core_peer, zh_peer, up, down] + x_peer + y_peer:
        pl.semaphore_signal(bar, inc=1, device_id=(peer, s), device_id_type=MESH)

    @pl.when(s > 0)
    def _():
        for peer in (d, zh_peer):
            pl.semaphore_signal(bar, inc=1, device_id=(peer, s - 1), device_id_type=MESH)

    @pl.when(s < 3)
    def _():
        for peer in (d, zh_peer):
            pl.semaphore_signal(bar, inc=1, device_id=(peer, s + 1), device_id_type=MESH)

    for copy in loads:
        copy.start()
    sides = jnp.where(s > 0, 2, 0) + jnp.where(s < 3, 2, 0)
    pl.semaphore_wait(bar, 10 + sides)

    loads[0].wait()

    def to_above():
        return pltpu.make_async_remote_copy(
            rot.at[3], rot_in.at[0], rot_s.at[0], rot_r.at[0], device_id=(d, s + 1), device_id_type=MESH)

    def to_below():
        return pltpu.make_async_remote_copy(
            rot.at[0], rot_in.at[1], rot_s.at[1], rot_r.at[1], device_id=(d, s - 1), device_id_type=MESH)

    @pl.when(s < 3)
    def _():
        to_above().start()

    @pl.when(s > 0)
    def _():
        to_below().start()

    zero_blk[...] = jnp.zeros_like(zero_blk)
    half[16] = jnp.zeros((256, 256), BF16)

    def flip(i, _):
        rot_t[i + 1] = rot[i].T
        return 0

    lax.fori_loop(0, 4, flip, 0)

    loads[1].wait()
    for p in range(4):
        loads[2 + p].wait()

        def stage_one(i, _, p=p):
            block = left[4 * p + i]
            w = pres[p, i].astype(F32)
            half[4 * p + i] = (jnp.dot(block, psi[i], preferred_element_type=F32) * w).astype(BF16)
            rotd[4 * p + i] = jnp.dot(block, rot[i], preferred_element_type=F32).astype(BF16)
            return 0

        lax.fori_loop(0, 4, stage_one, 0)

    kinds = [dirs[p, 0] for p in range(4)]
    fresh = []
    for p in range(4):
        seen = jnp.int32(0)
        for q in range(p):
            seen = seen + (kinds[q] == kinds[p]).astype(jnp.int32)
        fresh.append((seen == 0).astype(jnp.int32))
    first = {}
    for k in (1, 2, 3):
        pick = jnp.int32(0)
        for p in range(1, 4):
            pick = pick + p * fresh[p] * (kinds[p] == k).astype(jnp.int32)
        first[k] = pick
    extra = 6 - first[1] - first[2] - first[3]
    extra = jnp.clip(extra, 0, 3)
    extra_kind = dirs[extra, 0]

    @pl.when(s > 0)
    def _():
        to_above().wait_recv()
        rot_t[0] = rot_in[0].T

    @pl.when(s == 0)
    def _():
        rot_t[0] = jnp.zeros((256, 256), BF16)

    @pl.when(s < 3)
    def _():
        to_below().wait_recv()
        rot_t[5] = rot_in[1].T

    @pl.when(s == 3)
    def _():
        rot_t[5] = jnp.zeros((256, 256), BF16)

    def moved(k, j):
        to = {1: up, 2: down, 3: across}[k]
        n = 2 * (k - 1) + j
        return pltpu.make_async_remote_copy(
            pay.at[n], reg.at[2 * k + j], pay_s.at[n], pay_r.at[n], device_id=(to, s), device_id_type=MESH)

    def renormed(p, i):
        w = pres[p, i].astype(F32)
        return jnp.dot(rot_t[i + 1 + chg[p]], rotd[4 * p + i], preferred_element_type=F32) * w

    for k in (3, 1, 2):
        pair = first[k]

        def stage_two(i, _, pair=pair, k=k):
            pay[2 * (k - 1), i] = renormed(pair, i).astype(BF16)
            return 0

        lax.fori_loop(0, 4, stage_two, 0)
        moved(k, 0).start()

    def stage_three(i, _):
        block = renormed(extra, i)
        for k in (3, 1, 2):
            pay[2 * (k - 1) + 1, i] = (block * (extra_kind == k).astype(F32)).astype(BF16)
        pay[6, i] = (block * (extra_kind == 0).astype(F32)).astype(BF16)
        return 0

    lax.fori_loop(0, 4, stage_three, 0)
    for k in (3, 1, 2):
        moved(k, 1).start()
    stay = pltpu.make_async_copy(pay.at[6], reg.at[0], loc_sem.at[0])
    blank = pltpu.make_async_copy(zero_blk, reg.at[1], loc_sem.at[1])
    stay.start()
    blank.start()

    loads[6].wait()
    row = lax.broadcasted_iota(jnp.int32, (256, 256), 0)
    col = lax.broadcasted_iota(jnp.int32, (256, 256), 1)
    natural = ((row // 8) % 4) * 64 + ((row // 4) % 2) * 32 + ((row // 32) % 4) * 8 + (row // 128) * 4 + row % 4
    order = (col == natural).astype(BF16)

    def target_sum(e, _):
        total = jnp.zeros((256, 256), F32)
        for p in range(4):
            src = e - 1 - chg[p]
            inside = jnp.logical_and(src >= 0, src <= 3)
            clipped = jnp.clip(src, 0, 3)
            lhs = half[jnp.where(inside, 4 * p + clipped, 16)]
            total = total + lax.dot_general(lhs, right[4 * p + clipped], NT, preferred_element_type=F32)
        placed = jnp.dot(order, total.astype(BF16), preferred_element_type=F32).astype(BF16)
        part[e, 0] = placed[:128]
        part[e, 1] = placed[128:]
        return 0

    lax.fori_loop(0, 6, target_sum, 0)

    to_core = pltpu.make_async_remote_copy(
        part.at[:, 1 - c], c_in, c_s.at[0], c_r.at[0], device_id=(core_peer, s), device_id_type=MESH)
    to_core.start()
    to_core.wait()

    def core_sum(e, _):
        both = part[e, c].astype(F32) + c_in[e].astype(F32)
        x_out[e] = both.reshape(4, 32, 256).astype(BF16)
        return 0

    lax.fori_loop(0, 6, core_sum, 0)
    to_x = []
    for o in range(3):
        copy = pltpu.make_async_remote_copy(
            x_out.at[:, (x + o + 1) % 4], x_in.at[o], x_s.at[o], x_r.at[o],
            device_id=(x_peer[o], s), device_id_type=MESH)
        copy.start()
        to_x.append(copy)
    for copy in to_x:
        copy.wait()
    rows = pl.ds(pl.multiple_of(x * 32, 32), 32)

    def x_sum(e, _):
        total = part[e, c, rows].astype(F32) + c_in[e, rows].astype(F32)
        for o in range(3):
            total = total + x_in[o, e].astype(F32)
        for q in range(4):
            f2[q, e] = total[8 * q:8 * q + 8]
        return 0

    lax.fori_loop(0, 6, x_sum, 0)
    for q in range(4):
        y_out[q] = f2[q].reshape(48, 256).astype(BF16)
    to_y = []
    for o in range(3):
        copy = pltpu.make_async_remote_copy(
            y_out.at[(y + o + 1) % 4], y_in.at[o], y_s.at[o], y_r.at[o],
            device_id=(y_peer[o], s), device_id_type=MESH)
        copy.start()
        to_y.append(copy)
    for copy in to_y:
        copy.wait()
    total = f2[y].reshape(48, 256)
    for o in range(3):
        total = total + y_in[o].astype(F32)
    z_out[...] = total[8:40].astype(BF16)
    e_out[0] = total[0:8]
    e_out[1] = total[40:48]
    to_z = pltpu.make_async_remote_copy(
        z_out, z_in, z_s.at[0], z_r.at[0], device_id=(zh_peer, s), device_id_type=MESH)
    to_z.start()

    def edge(side, far):
        op_to = zh_peer if far else d
        sec_to = s + 1 if side else s - 1
        return pltpu.make_async_remote_copy(
            e_out.at[side], e_in.at[side, far], e_s.at[side, far], e_r.at[side, far],
            device_id=(op_to, sec_to), device_id_type=MESH)

    @pl.when(s < 3)
    def _():
        edge(1, 0).start()
        edge(1, 1).start()

    @pl.when(s > 0)
    def _():
        edge(0, 0).start()
        edge(0, 1).start()

    to_z.wait()
    mine = (total[8:40] + z_in[...].astype(F32)).reshape(4, 8, 256)
    f2[0, pl.ds(0, 4)] = mine

    @pl.when(s > 0)
    def _():
        edge(1, 0).wait_recv()
        edge(1, 1).wait_recv()
        f2[0, 0] = f2[0, 0] + e_in[1, 0] + e_in[1, 1]

    @pl.when(s < 3)
    def _():
        edge(0, 0).wait_recv()
        edge(0, 1).wait_recv()
        f2[0, 3] = f2[0, 3] + e_in[0, 0] + e_in[0, 1]

    final = f2[0, pl.ds(0, 4)] * (1.0 / 16.0)
    sig[...] = jnp.where(zh == 0, final[:, 0:4], final[:, 4:8])

    @pl.when(s < 3)
    def _():
        edge(1, 0).wait_send()
        edge(1, 1).wait_send()
        to_above().wait_send()

    @pl.when(s > 0)
    def _():
        edge(0, 0).wait_send()
        edge(0, 1).wait_send()
        to_below().wait_send()

    for k in (3, 1, 2):
        for j in (0, 1):
            moved(k, j).wait()
    stay.wait()
    blank.wait()


def body(wavefunction, left_operators, right_operators, rotations, charges, present_blocks, directions):
    hbm = pl.BlockSpec(memory_space=pltpu.HBM)
    smem = pl.BlockSpec(memory_space=pltpu.SMEM)
    dma = pltpu.SemaphoreType.DMA
    sigma, regrouped = pl.pallas_call(
        kernel,
        out_shape=(
            jax.ShapeDtypeStruct((4, 4, 256), F32),
            jax.ShapeDtypeStruct((8, 4, 256, 256), BF16),
        ),
        in_specs=[smem, smem, smem, hbm, hbm, hbm, hbm],
        out_specs=(pl.BlockSpec(memory_space=pltpu.VMEM), hbm),
        scratch_shapes=[
            pltpu.VMEM((4, 256, 256), BF16),
            pltpu.VMEM((16, 256, 256), BF16),
            pltpu.VMEM((16, 256, 256), BF16),
            pltpu.VMEM((4, 256, 256), BF16),
            pltpu.VMEM((6, 256, 256), BF16),
            pltpu.VMEM((2, 256, 256), BF16),
            pltpu.VMEM((17, 256, 256), BF16),
            pltpu.VMEM((16, 256, 256), BF16),
            pltpu.VMEM((7, 4, 256, 256), BF16),
            pltpu.VMEM((4, 256, 256), BF16),
            pltpu.VMEM((6, 2, 128, 256), BF16),
            pltpu.VMEM((6, 128, 256), BF16),
            pltpu.VMEM((6, 4, 32, 256), BF16),
            pltpu.VMEM((3, 6, 32, 256), BF16),
            pltpu.VMEM((4, 6, 8, 256), F32),
            pltpu.VMEM((4, 48, 256), BF16),
            pltpu.VMEM((3, 48, 256), BF16),
            pltpu.VMEM((32, 256), BF16),
            pltpu.VMEM((32, 256), BF16),
            pltpu.VMEM((2, 8, 256), F32),
            pltpu.VMEM((2, 2, 8, 256), F32),
            dma((7,)), dma((2,)), dma((2,)), dma((6,)), dma((6,)), dma((2,)),
            dma((1,)), dma((1,)), dma((3,)), dma((3,)), dma((3,)), dma((3,)),
            dma((1,)), dma((1,)), dma((2, 2)), dma((2, 2)),
        ],
        compiler_params=pltpu.CompilerParams(
            collective_id=0, has_side_effects=True, vmem_limit_bytes=48 * 1024 * 1024),
        name="step",
    )(
        charges, present_blocks, directions,
        wavefunction,
        left_operators.reshape(16, 256, 256),
        right_operators.reshape(16, 256, 256),
        rotations,
    )
    return sigma, regrouped


def solution(mesh):
    placed = (
        P("sec", None, None),
        P("op", "sec", None, None),
        P("op", "sec", None, None),
        P("sec", None, None),
        P("op"),
        P("op", "sec"),
        P("op", None),
    )
    return jax.shard_map(
        body,
        mesh=mesh,
        in_specs=placed,
        out_specs=(P("sec", "op", None), P("op", "sec", None, None)),
        check_vma=False,
    )
```

```python
import jax
import jax.numpy as jnp
from jax import lax
from jax.experimental import pallas as pl
from jax.experimental.pallas import tpu as pltpu
from jax.sharding import PartitionSpec as P

MESH = pl.DeviceIdType.MESH
F32 = jnp.float32
BF16 = jnp.bfloat16
NT = (((1,), (1,)), ((), ()))


def place(y, zh, x, c):
    return y * 16 + zh * 8 + x * 2 + c


def kernel(
    chg, pres, dirs, psi_h, left_h, right_h, rot_h,
    sig, reg,
    psi, left, right, rot, rot_t, rot_in, half, rotd, pay,
    part, c_in, x_out, x_in, f2, y_out, y_in, z_out, z_in, e_out, e_in,
    in_sem, rot_s, rot_r, pay_s, pay_r, c_s, c_r, x_s, x_r, y_s, y_r, z_s, z_r, e_s, e_r,
):
    d = lax.axis_index("op")
    s = lax.axis_index("sec")
    y, zh, x, c = d // 16, (d // 8) % 2, (d // 2) % 4, d % 2
    core_peer = place(y, zh, x, 1 - c)
    x_peer = [place(y, zh, (x + o) % 4, c) for o in (1, 2, 3)]
    y_peer = [place((y + o) % 4, zh, x, c) for o in (1, 2, 3)]
    zh_peer = place(y, 1 - zh, x, c)
    up, down, across = (d + 1) % 64, (d + 63) % 64, (d + 32) % 64

    loads = [
        pltpu.make_async_copy(rot_h, rot, in_sem.at[0]),
        pltpu.make_async_copy(psi_h, psi, in_sem.at[1]),
    ]
    for p in range(4):
        loads.append(pltpu.make_async_copy(left_h.at[pl.ds(4 * p, 4)], left.at[pl.ds(4 * p, 4)], in_sem.at[2 + p]))
    loads.append(pltpu.make_async_copy(right_h, right, in_sem.at[6]))

    bar = pltpu.get_barrier_semaphore()
    for peer in [core_peer, zh_peer, up, down] + x_peer + y_peer:
        pl.semaphore_signal(bar, inc=1, device_id=(peer, s), device_id_type=MESH)

    @pl.when(s > 0)
    def _():
        for peer in (d, zh_peer):
            pl.semaphore_signal(bar, inc=1, device_id=(peer, s - 1), device_id_type=MESH)

    @pl.when(s < 3)
    def _():
        for peer in (d, zh_peer):
            pl.semaphore_signal(bar, inc=1, device_id=(peer, s + 1), device_id_type=MESH)

    for copy in loads:
        copy.start()
    loads[0].wait()
    half[16] = jnp.zeros((256, 256), BF16)

    def flip(i, _):
        rot_t[i + 1] = rot[i].T
        return 0

    lax.fori_loop(0, 4, flip, 0)
    rot_t[0] = jnp.zeros((256, 256), BF16)
    rot_t[5] = jnp.zeros((256, 256), BF16)
    reg[1] = jnp.zeros((4, 256, 256), BF16)

    loads[1].wait()
    for p in range(4):
        loads[2 + p].wait()

        def stage_one(i, _, p=p):
            block = left[4 * p + i]
            w = pres[p, i].astype(F32)
            half[4 * p + i] = (jnp.dot(block, psi[i], preferred_element_type=F32) * w).astype(BF16)
            rotd[4 * p + i] = jnp.dot(block, rot[i], preferred_element_type=F32).astype(BF16)
            return 0

        lax.fori_loop(0, 4, stage_one, 0)

    kinds = [dirs[p] for p in range(4)]
    fresh = []
    for p in range(4):
        seen = jnp.int32(0)
        for q in range(p):
            seen = seen + (kinds[q] == kinds[p]).astype(jnp.int32)
        fresh.append((seen == 0).astype(jnp.int32))
    first = {}
    for k in (1, 2, 3):
        pick = jnp.int32(0)
        for p in range(1, 4):
            pick = pick + p * fresh[p] * (kinds[p] == k).astype(jnp.int32)
        first[k] = pick
    extra = 6 - first[1] - first[2] - first[3]
    extra = jnp.clip(extra, 0, 3)
    extra_kind = dirs[extra]

    sides = jnp.where(s > 0, 2, 0) + jnp.where(s < 3, 2, 0)
    pl.semaphore_wait(bar, 10 + sides)

    def to_above():
        return pltpu.make_async_remote_copy(
            rot.at[3], rot_in.at[0], rot_s.at[0], rot_r.at[0], device_id=(d, s + 1), device_id_type=MESH)

    def to_below():
        return pltpu.make_async_remote_copy(
            rot.at[0], rot_in.at[1], rot_s.at[1], rot_r.at[1], device_id=(d, s - 1), device_id_type=MESH)

    @pl.when(s < 3)
    def _():
        to_above().start()

    @pl.when(s > 0)
    def _():
        to_below().start()


    def moved(k, j, part_no):
        to = {1: up, 2: down, 3: across}[k]
        n = 2 * (k - 1) + j
        cut = (pl.ds(0, 1), pl.ds(1, 2), pl.ds(3, 1))[part_no]
        return pltpu.make_async_remote_copy(
            pay.at[n, cut], reg.at[2 * k + j, cut], pay_s.at[n, part_no], pay_r.at[n, part_no],
            device_id=(to, s), device_id_type=MESH)

    def renormed(p, i):
        w = pres[p, i].astype(F32)
        return jnp.dot(rot_t[i + 1 + chg[p]], rotd[4 * p + i], preferred_element_type=F32) * w

    def firsts(k, i):
        pay[2 * (k - 1), i] = renormed(first[k], i).astype(BF16)

    def extras(i):
        block = renormed(extra, i)
        for k in (1, 2, 3):
            pay[2 * (k - 1) + 1, i] = (block * (extra_kind == k).astype(F32)).astype(BF16)
        reg[0, i] = (block * (extra_kind == 0).astype(F32)).astype(BF16)

    for k in (1, 2, 3):
        def inner(i, _, k=k):
            firsts(k, i)
            return 0

        lax.fori_loop(1, 3, inner, 0)
        moved(k, 0, 1).start()

    def inner_extra(i, _):
        extras(i)
        return 0

    lax.fori_loop(1, 3, inner_extra, 0)
    for k in (1, 2, 3):
        moved(k, 1, 1).start()

    loads[6].wait()
    row = lax.broadcasted_iota(jnp.int32, (256, 256), 0)
    col = lax.broadcasted_iota(jnp.int32, (256, 256), 1)
    natural = ((row // 8) % 4) * 64 + ((row // 4) % 2) * 32 + ((row // 32) % 4) * 8 + (row // 128) * 4 + row % 4
    order = (col == natural).astype(BF16)

    def target_sum(e, _):
        total = jnp.zeros((256, 256), F32)
        for p in range(4):
            src = e - 1 - chg[p]
            inside = jnp.logical_and(src >= 0, src <= 3)
            clipped = jnp.clip(src, 0, 3)
            lhs = half[jnp.where(inside, 4 * p + clipped, 16)]
            total = total + lax.dot_general(lhs, right[4 * p + clipped], NT, preferred_element_type=F32)
        placed = jnp.dot(order, total.astype(BF16), preferred_element_type=F32).astype(BF16)
        part[e, 0] = placed[:128]
        part[e, 1] = placed[128:]
        return 0

    lax.fori_loop(0, 6, target_sum, 0)

    to_core = pltpu.make_async_remote_copy(
        part.at[:, 1 - c], c_in, c_s.at[0], c_r.at[0], device_id=(core_peer, s), device_id_type=MESH)
    to_core.start()

    @pl.when(s > 0)
    def _():
        to_above().wait_recv()
        rot_t[0] = rot_in[0].T

    @pl.when(s < 3)
    def _():
        to_below().wait_recv()
        rot_t[5] = rot_in[1].T

    def outer(q, _):
        for k in (1, 2, 3):
            firsts(k, 3 * q)
        extras(3 * q)
        return 0

    lax.fori_loop(0, 2, outer, 0)

    def send_outer(k):
        for j in (0, 1):
            for part_no in (0, 2):
                moved(k, j, part_no).start()

    far_up = jnp.logical_and(x == 3, c == 1)
    far_down = jnp.logical_and(x == 0, c == 0)
    to_core.wait_recv()

    def core_sum(e, _):
        both = part[e, c].astype(F32) + c_in[e].astype(F32)
        x_out[e] = both.reshape(4, 32, 256).astype(BF16)
        return 0

    lax.fori_loop(0, 6, core_sum, 0)
    to_x = []
    for o in range(3):
        copy = pltpu.make_async_remote_copy(
            x_out.at[:, (x + o + 1) % 4], x_in.at[o], x_s.at[o], x_r.at[o],
            device_id=(x_peer[o], s), device_id_type=MESH)
        copy.start()
        to_x.append(copy)

    @pl.when(jnp.logical_not(far_up))
    def _():
        send_outer(1)

    @pl.when(jnp.logical_not(far_down))
    def _():
        send_outer(2)

    for copy in to_x:
        copy.wait_recv()
    rows = pl.ds(pl.multiple_of(x * 32, 32), 32)

    def x_sum(e, _):
        total = part[e, c, rows].astype(F32) + c_in[e, rows].astype(F32)
        for o in range(3):
            total = total + x_in[o, e].astype(F32)
        for q in range(4):
            f2[q, e] = total[8 * q:8 * q + 8]
        return 0

    lax.fori_loop(0, 6, x_sum, 0)
    for q in range(4):
        y_out[q] = f2[q].reshape(48, 256).astype(BF16)
    to_y = []
    for o in range(3):
        copy = pltpu.make_async_remote_copy(
            y_out.at[(y + o + 1) % 4], y_in.at[o], y_s.at[o], y_r.at[o],
            device_id=(y_peer[o], s), device_id_type=MESH)
        copy.start()
        to_y.append(copy)
    send_outer(3)
    for copy in to_y:
        copy.wait_recv()
    total = f2[y].reshape(48, 256)
    for o in range(3):
        total = total + y_in[o].astype(F32)
    z_out[...] = total[8:40].astype(BF16)
    e_out[0] = total[0:8]
    e_out[1] = total[40:48]
    to_z = pltpu.make_async_remote_copy(
        z_out, z_in, z_s.at[0], z_r.at[0], device_id=(zh_peer, s), device_id_type=MESH)
    to_z.start()

    def edge(side, far):
        op_to = zh_peer if far else d
        sec_to = s + 1 if side else s - 1
        return pltpu.make_async_remote_copy(
            e_out.at[side], e_in.at[side, far], e_s.at[side, far], e_r.at[side, far],
            device_id=(op_to, sec_to), device_id_type=MESH)

    @pl.when(s < 3)
    def _():
        edge(1, 0).start()
        edge(1, 1).start()

    @pl.when(s > 0)
    def _():
        edge(0, 0).start()
        edge(0, 1).start()

    @pl.when(far_up)
    def _():
        send_outer(1)

    @pl.when(far_down)
    def _():
        send_outer(2)

    to_z.wait_recv()
    mine = (total[8:40] + z_in[...].astype(F32)).reshape(4, 8, 256)
    f2[0, pl.ds(0, 4)] = mine

    @pl.when(s > 0)
    def _():
        edge(1, 0).wait_recv()
        edge(1, 1).wait_recv()
        f2[0, 0] = f2[0, 0] + e_in[1, 0] + e_in[1, 1]

    @pl.when(s < 3)
    def _():
        edge(0, 0).wait_recv()
        edge(0, 1).wait_recv()
        f2[0, 3] = f2[0, 3] + e_in[0, 0] + e_in[0, 1]

    final = f2[0, pl.ds(0, 4)] * (1.0 / 16.0)
    sig[...] = jnp.where(zh == 0, final[:, 0:4], final[:, 4:8])

    for copy in [to_core, to_z] + to_x + to_y:
        copy.wait_send()

    @pl.when(s < 3)
    def _():
        edge(1, 0).wait_send()
        edge(1, 1).wait_send()
        to_above().wait_send()

    @pl.when(s > 0)
    def _():
        edge(0, 0).wait_send()
        edge(0, 1).wait_send()
        to_below().wait_send()

    for k in (1, 2, 3):
        for j in (0, 1):
            for part_no in range(3):
                moved(k, j, part_no).wait()


def body(wavefunction, left_operators, right_operators, rotations, charges, present_blocks, directions):
    hbm = pl.BlockSpec(memory_space=pltpu.HBM)
    vmem = pl.BlockSpec(memory_space=pltpu.VMEM)
    smem = pl.BlockSpec(memory_space=pltpu.SMEM)
    dma = pltpu.SemaphoreType.DMA
    sigma, regrouped = pl.pallas_call(
        kernel,
        out_shape=(
            pltpu.VMEM((4, 4, 256), F32),
            pltpu.VMEM((8, 4, 256, 256), BF16),
        ),
        in_specs=[smem, smem, smem, hbm, hbm, hbm, hbm],
        out_specs=(vmem, vmem),
        scratch_shapes=[
            pltpu.VMEM((4, 256, 256), BF16),
            pltpu.VMEM((16, 256, 256), BF16),
            pltpu.VMEM((16, 256, 256), BF16),
            pltpu.VMEM((4, 256, 256), BF16),
            pltpu.VMEM((6, 256, 256), BF16),
            pltpu.VMEM((2, 256, 256), BF16),
            pltpu.VMEM((17, 256, 256), BF16),
            pltpu.VMEM((16, 256, 256), BF16),
            pltpu.VMEM((6, 4, 256, 256), BF16),
            pltpu.VMEM((6, 2, 128, 256), BF16),
            pltpu.VMEM((6, 128, 256), BF16),
            pltpu.VMEM((6, 4, 32, 256), BF16),
            pltpu.VMEM((3, 6, 32, 256), BF16),
            pltpu.VMEM((4, 6, 8, 256), F32),
            pltpu.VMEM((4, 48, 256), BF16),
            pltpu.VMEM((3, 48, 256), BF16),
            pltpu.VMEM((32, 256), BF16),
            pltpu.VMEM((32, 256), BF16),
            pltpu.VMEM((2, 8, 256), F32),
            pltpu.VMEM((2, 2, 8, 256), F32),
            dma((7,)), dma((2,)), dma((2,)), dma((6, 3)), dma((6, 3)),
            dma((1,)), dma((1,)), dma((3,)), dma((3,)), dma((3,)), dma((3,)),
            dma((1,)), dma((1,)), dma((2, 2)), dma((2, 2)),
        ],
        compiler_params=pltpu.CompilerParams(
            collective_id=0, has_side_effects=True, vmem_limit_bytes=58000000),
        name="step",
    )(
        charges, present_blocks, directions.reshape(4),
        wavefunction,
        left_operators.reshape(16, 256, 256),
        right_operators.reshape(16, 256, 256),
        rotations,
    )
    return sigma, regrouped


def solution(mesh):
    placed = (
        P("sec", None, None),
        P("op", "sec", None, None),
        P("op", "sec", None, None),
        P("sec", None, None),
        P("op"),
        P("op", "sec"),
        P("op", None),
    )
    return jax.shard_map(
        body,
        mesh=mesh,
        in_specs=placed,
        out_specs=(P("sec", "op", None), P("op", "sec", None, None)),
        check_vma=False,
    )
```

```python
import jax
import jax.numpy as jnp
from jax import lax
from jax.experimental import pallas as pl
from jax.experimental.pallas import tpu as pltpu
from jax.sharding import PartitionSpec as P

MESH = pl.DeviceIdType.MESH
F32 = jnp.float32
BF16 = jnp.bfloat16
NT = (((1,), (1,)), ((), ()))


def place(y, zh, x, c):
    return y * 16 + zh * 8 + x * 2 + c


def kernel(
    chg, pres, dirs, psi_h, left_h, right_h, rot_h,
    sig, reg,
    psi, left, right, rot, rot_t, rot_in, half, rotd, pay, hand,
    part, c_in, x_out, x_in, f2, y_out, y_in, z_out, z_in, e_out, e_in,
    in_sem, rot_s, rot_r, pay_s, pay_r, hand_s, hand_r, c_s, c_r, x_s, x_r, y_s, y_r, z_s, z_r, e_s, e_r,
):
    d = lax.axis_index("op")
    s = lax.axis_index("sec")
    y, zh, x, c = d // 16, (d // 8) % 2, (d // 2) % 4, d % 2
    core_peer = place(y, zh, x, 1 - c)
    x_peer = [place(y, zh, (x + o) % 4, c) for o in (1, 2, 3)]
    y_peer = [place((y + o) % 4, zh, x, c) for o in (1, 2, 3)]
    zh_peer = place(y, 1 - zh, x, c)
    up, down, across = (d + 1) % 64, (d + 63) % 64, (d + 32) % 64

    far_up = jnp.logical_and(x == 3, c == 1)
    far_down = jnp.logical_and(x == 0, c == 0)
    hand_up = jnp.logical_and(x == 2, c == 0)
    hand_down = jnp.logical_and(x == 1, c == 1)
    via_up = place((y + zh) % 4, zh, 2, 0)
    via_down = place((y + 3 + zh) % 4, zh, 1, 1)
    late_up = place(y, 1 - zh, 2, 0)
    late_down = place(y, 1 - zh, 1, 1)
    from_up = place((y + 4 - zh) % 4, zh, 3, 1)
    from_down = place((y + 1 - zh) % 4, zh, 0, 0)
    onto_up = place(y, 1 - zh, 0, 0)
    onto_down = place(y, 1 - zh, 3, 1)

    loads = [pltpu.make_async_copy(rot_h, rot, in_sem.at[0])]
    for p in range(4):
        loads.append(pltpu.make_async_copy(left_h.at[pl.ds(4 * p, 4)], left.at[pl.ds(4 * p, 4)], in_sem.at[1 + p]))
    loads.append(pltpu.make_async_copy(psi_h, psi, in_sem.at[5]))
    loads.append(pltpu.make_async_copy(right_h, right, in_sem.at[6]))

    bar = pltpu.get_barrier_semaphore()
    for peer in [core_peer, zh_peer, up, down] + x_peer + y_peer:
        pl.semaphore_signal(bar, inc=1, device_id=(peer, s), device_id_type=MESH)

    @pl.when(s > 0)
    def _():
        for peer in (d, zh_peer):
            pl.semaphore_signal(bar, inc=1, device_id=(peer, s - 1), device_id_type=MESH)

    @pl.when(s < 3)
    def _():
        for peer in (d, zh_peer):
            pl.semaphore_signal(bar, inc=1, device_id=(peer, s + 1), device_id_type=MESH)

    def greet(when, peers):
        @pl.when(when)
        def _():
            for peer in peers:
                pl.semaphore_signal(bar, inc=1, device_id=(peer, s), device_id_type=MESH)

    greet(far_up, (via_up, late_down))
    greet(far_down, (via_down, late_up))
    greet(hand_up, (from_up, onto_up))
    greet(hand_down, (from_down, onto_down))

    for copy in loads:
        copy.start()
    loads[0].wait()
    half[16] = jnp.zeros((256, 256), BF16)

    def flip(i, _):
        rot_t[i + 1] = rot[i].T
        return 0

    lax.fori_loop(0, 4, flip, 0)
    rot_t[0] = jnp.zeros((256, 256), BF16)
    rot_t[5] = jnp.zeros((256, 256), BF16)
    reg[1] = jnp.zeros((4, 256, 256), BF16)

    for p in range(4):
        loads[1 + p].wait()

    def rotate(p, i):
        rotd[4 * p + i] = jnp.dot(left[4 * p + i], rot[i], preferred_element_type=F32).astype(BF16)

    def rotate_inner(p, _):
        rotate(p, 1)
        rotate(p, 2)
        return 0

    lax.fori_loop(0, 4, rotate_inner, 0)

    kinds = [dirs[p] for p in range(4)]
    fresh = []
    for p in range(4):
        seen = jnp.int32(0)
        for q in range(p):
            seen = seen + (kinds[q] == kinds[p]).astype(jnp.int32)
        fresh.append((seen == 0).astype(jnp.int32))
    first = {}
    for k in (1, 2, 3):
        pick = jnp.int32(0)
        for p in range(1, 4):
            pick = pick + p * fresh[p] * (kinds[p] == k).astype(jnp.int32)
        first[k] = pick
    extra = 6 - first[1] - first[2] - first[3]
    extra = jnp.clip(extra, 0, 3)
    extra_kind = dirs[extra]

    def to_above():
        return pltpu.make_async_remote_copy(
            rot.at[3], rot_in.at[0], rot_s.at[0], rot_r.at[0], device_id=(d, s + 1), device_id_type=MESH)

    def to_below():
        return pltpu.make_async_remote_copy(
            rot.at[0], rot_in.at[1], rot_s.at[1], rot_r.at[1], device_id=(d, s - 1), device_id_type=MESH)

    def moved(k, j, i):
        to = {1: up, 2: down, 3: across}[k]
        n = 2 * (k - 1) + j
        return pltpu.make_async_remote_copy(
            pay.at[n, i], reg.at[2 * k + j, i], pay_s.at[n, i], pay_r.at[n, i],
            device_id=(to, s), device_id_type=MESH)

    def to_hand(k, j, i):
        n, h = 2 * (k - 1) + j, 2 * (i - 1) + j
        return pltpu.make_async_remote_copy(
            pay.at[n, i], hand.at[h], pay_s.at[n, i], hand_r.at[h],
            device_id=({1: via_up, 2: via_down}[k], s), device_id_type=MESH)

    def from_hand(k, j, i):
        n, h = 2 * (k - 1) + j, 2 * (i - 1) + j
        return pltpu.make_async_remote_copy(
            hand.at[h], reg.at[2 * k + j, i], hand_s.at[h], pay_r.at[n, i],
            device_id=({1: onto_up, 2: onto_down}[k], s), device_id_type=MESH)

    def send_far(sectors):
        for k, far in ((1, far_up), (2, far_down)):
            @pl.when(far)
            def _(k=k):
                for i in sectors:
                    for j in (0, 1):
                        (to_hand if i in (1, 2) else moved)(k, j, i).start()

    def send_beside(sectors):
        for k, here in ((1, c == 0), (2, c == 1)):
            @pl.when(here)
            def _(k=k):
                for i in sectors:
                    for j in (0, 1):
                        moved(k, j, i).start()

    def send_ring(sectors):
        for k, here in ((1, (c == 1) & (x < 3)), (2, (c == 0) & (x > 0))):
            @pl.when(here)
            def _(k=k):
                for i in sectors:
                    for j in (0, 1):
                        moved(k, j, i).start()

    def send_across(sectors):
        for i in sectors:
            for j in (0, 1):
                moved(3, j, i).start()

    def hand_on():
        for k, here in ((1, hand_up), (2, hand_down)):
            @pl.when(here)
            def _(k=k):
                for i in (1, 2):
                    for j in (0, 1):
                        to_hand(k, j, i).wait_recv()
                        from_hand(k, j, i).start()

    def renormed(p, i):
        w = pres[p, i].astype(F32)
        return jnp.dot(rot_t[i + 1 + chg[p]], rotd[4 * p + i], preferred_element_type=F32) * w

    def firsts(k, i):
        pay[2 * (k - 1), i] = renormed(first[k], i).astype(BF16)

    def extras(i):
        block = renormed(extra, i)
        for k in (1, 2, 3):
            pay[2 * (k - 1) + 1, i] = (block * (extra_kind == k).astype(F32)).astype(BF16)
        reg[0, i] = (block * (extra_kind == 0).astype(F32)).astype(BF16)

    def all_of(i):
        for k in (1, 2, 3):
            firsts(k, i)
        extras(i)

    def inner(i, _):
        all_of(i)
        return 0

    lax.fori_loop(1, 3, inner, 0)
    sides = jnp.where(s > 0, 2, 0) + jnp.where(s < 3, 2, 0)
    corner = far_up | far_down | hand_up | hand_down
    pl.semaphore_wait(bar, 10 + sides + jnp.where(corner, 2, 0))

    @pl.when(s < 3)
    def _():
        to_above().start()

    @pl.when(s > 0)
    def _():
        to_below().start()

    send_far((1, 2))
    send_across((1, 2))
    send_beside((1, 2))

    loads[5].wait()

    def halve(p, _):
        for i in range(4):
            w = pres[p, i].astype(F32)
            half[4 * p + i] = (jnp.dot(left[4 * p + i], psi[i], preferred_element_type=F32) * w).astype(BF16)
        return 0

    lax.fori_loop(0, 4, halve, 0)

    def rotate_outer(p, _):
        rotate(p, 0)
        rotate(p, 3)
        return 0

    lax.fori_loop(0, 4, rotate_outer, 0)

    @pl.when(s > 0)
    def _():
        to_above().wait_recv()
        rot_t[0] = rot_in[0].T

    @pl.when(s < 3)
    def _():
        to_below().wait_recv()
        rot_t[5] = rot_in[1].T

    def outer(q, _):
        all_of(3 * q)
        return 0

    lax.fori_loop(0, 2, outer, 0)
    send_far((0, 3))
    send_across((0, 3))
    loads[6].wait()
    row = lax.broadcasted_iota(jnp.int32, (256, 256), 0)
    col = lax.broadcasted_iota(jnp.int32, (256, 256), 1)
    natural = ((row // 8) % 4) * 64 + ((row // 4) % 2) * 32 + ((row // 32) % 4) * 8 + (row // 128) * 4 + row % 4
    order = (col == natural).astype(BF16)

    def target_sum(e, _):
        total = jnp.zeros((256, 256), F32)
        for p in range(4):
            src = e - 1 - chg[p]
            inside = jnp.logical_and(src >= 0, src <= 3)
            clipped = jnp.clip(src, 0, 3)
            lhs = half[jnp.where(inside, 4 * p + clipped, 16)]
            total = total + lax.dot_general(lhs, right[4 * p + clipped], NT, preferred_element_type=F32)
        placed = jnp.dot(order, total.astype(BF16), preferred_element_type=F32).astype(BF16)
        part[e, 0] = placed[:128]
        part[e, 1] = placed[128:]
        return 0

    def to_core(g):
        some = pl.ds(3 * g, 3)
        return pltpu.make_async_remote_copy(
            part.at[some, 1 - c], c_in.at[some], c_s.at[g], c_r.at[g], device_id=(core_peer, s), device_id_type=MESH)

    def to_x(g, o):
        some = pl.ds(3 * g, 3)
        return pltpu.make_async_remote_copy(
            x_out.at[some, (x + o + 1) % 4], x_in.at[o, some], x_s.at[g, o], x_r.at[g, o],
            device_id=(x_peer[o], s), device_id_type=MESH)

    for g in (0, 1):
        lax.fori_loop(3 * g, 3 * g + 3, target_sum, 0)
        to_core(g).start()

    def core_sum(e, _):
        both = part[e, c].astype(F32) + c_in[e].astype(F32)
        x_out[e] = both.reshape(4, 32, 256).astype(BF16)
        return 0

    for g in (0, 1):
        to_core(g).wait_recv()
        lax.fori_loop(3 * g, 3 * g + 3, core_sum, 0)
        for o in range(3):
            to_x(g, o).start()
    hand_on()
    send_beside((0, 3))
    send_ring((0, 1, 2, 3))
    for g in (0, 1):
        for o in range(3):
            to_x(g, o).wait_recv()
    rows = pl.ds(pl.multiple_of(x * 32, 32), 32)

    def x_sum(e, _):
        total = part[e, c, rows].astype(F32) + c_in[e, rows].astype(F32)
        for o in range(3):
            total = total + x_in[o, e].astype(F32)
        for q in range(4):
            f2[q, e] = total[8 * q:8 * q + 8]
        return 0

    lax.fori_loop(0, 6, x_sum, 0)
    for q in range(4):
        y_out[q] = f2[q].reshape(48, 256).astype(BF16)
    to_y = []
    for o in range(3):
        copy = pltpu.make_async_remote_copy(
            y_out.at[(y + o + 1) % 4], y_in.at[o], y_s.at[o], y_r.at[o],
            device_id=(y_peer[o], s), device_id_type=MESH)
        copy.start()
        to_y.append(copy)
    for copy in to_y:
        copy.wait_recv()
    total = f2[y].reshape(48, 256)
    for o in range(3):
        total = total + y_in[o].astype(F32)
    z_out[...] = total[8:40].astype(BF16)
    e_out[0] = total[0:8]
    e_out[1] = total[40:48]
    to_z = pltpu.make_async_remote_copy(
        z_out, z_in, z_s.at[0], z_r.at[0], device_id=(zh_peer, s), device_id_type=MESH)
    to_z.start()

    def edge(side, far):
        op_to = zh_peer if far else d
        sec_to = s + 1 if side else s - 1
        return pltpu.make_async_remote_copy(
            e_out.at[side], e_in.at[side, far], e_s.at[side, far], e_r.at[side, far],
            device_id=(op_to, sec_to), device_id_type=MESH)

    @pl.when(s < 3)
    def _():
        edge(1, 0).start()
        edge(1, 1).start()

    @pl.when(s > 0)
    def _():
        edge(0, 0).start()
        edge(0, 1).start()

    to_z.wait_recv()
    mine = (total[8:40] + z_in[...].astype(F32)).reshape(4, 8, 256)
    f2[0, pl.ds(0, 4)] = mine

    @pl.when(s > 0)
    def _():
        edge(1, 0).wait_recv()
        edge(1, 1).wait_recv()
        f2[0, 0] = f2[0, 0] + e_in[1, 0] + e_in[1, 1]

    @pl.when(s < 3)
    def _():
        edge(0, 0).wait_recv()
        edge(0, 1).wait_recv()
        f2[0, 3] = f2[0, 3] + e_in[0, 0] + e_in[0, 1]

    final = f2[0, pl.ds(0, 4)] * (1.0 / 16.0)
    sig[...] = jnp.where(zh == 0, final[:, 0:4], final[:, 4:8])

    for copy in [to_z] + to_y:
        copy.wait_send()
    for g in (0, 1):
        to_core(g).wait_send()
        for o in range(3):
            to_x(g, o).wait_send()

    @pl.when(s < 3)
    def _():
        edge(1, 0).wait_send()
        edge(1, 1).wait_send()
        to_above().wait_send()

    @pl.when(s > 0)
    def _():
        edge(0, 0).wait_send()
        edge(0, 1).wait_send()
        to_below().wait_send()

    for k, here in ((1, hand_up), (2, hand_down)):
        @pl.when(here)
        def _(k=k):
            for j in (0, 1):
                for i in (1, 2):
                    from_hand(k, j, i).wait_send()

    for k in (1, 2, 3):
        for j in (0, 1):
            for i in range(4):
                moved(k, j, i).wait()


def body(wavefunction, left_operators, right_operators, rotations, charges, present_blocks, directions):
    hbm = pl.BlockSpec(memory_space=pltpu.HBM)
    vmem = pl.BlockSpec(memory_space=pltpu.VMEM)
    smem = pl.BlockSpec(memory_space=pltpu.SMEM)
    dma = pltpu.SemaphoreType.DMA
    sigma, regrouped = pl.pallas_call(
        kernel,
        out_shape=(
            pltpu.VMEM((4, 4, 256), F32),
            pltpu.VMEM((8, 4, 256, 256), BF16),
        ),
        in_specs=[smem, smem, smem, hbm, hbm, hbm, hbm],
        out_specs=(vmem, vmem),
        scratch_shapes=[
            pltpu.VMEM((4, 256, 256), BF16),
            pltpu.VMEM((16, 256, 256), BF16),
            pltpu.VMEM((16, 256, 256), BF16),
            pltpu.VMEM((4, 256, 256), BF16),
            pltpu.VMEM((6, 256, 256), BF16),
            pltpu.VMEM((2, 256, 256), BF16),
            pltpu.VMEM((17, 256, 256), BF16),
            pltpu.VMEM((16, 256, 256), BF16),
            pltpu.VMEM((6, 4, 256, 256), BF16),
            pltpu.VMEM((4, 256, 256), BF16),
            pltpu.VMEM((6, 2, 128, 256), BF16),
            pltpu.VMEM((6, 128, 256), BF16),
            pltpu.VMEM((6, 4, 32, 256), BF16),
            pltpu.VMEM((3, 6, 32, 256), BF16),
            pltpu.VMEM((4, 6, 8, 256), F32),
            pltpu.VMEM((4, 48, 256), BF16),
            pltpu.VMEM((3, 48, 256), BF16),
            pltpu.VMEM((32, 256), BF16),
            pltpu.VMEM((32, 256), BF16),
            pltpu.VMEM((2, 8, 256), F32),
            pltpu.VMEM((2, 2, 8, 256), F32),
            dma((7,)), dma((2,)), dma((2,)), dma((6, 4)), dma((6, 4)), dma((4,)), dma((4,)),
            dma((2,)), dma((2,)), dma((2, 3)), dma((2, 3)), dma((3,)), dma((3,)),
            dma((1,)), dma((1,)), dma((2, 2)), dma((2, 2)),
        ],
        compiler_params=pltpu.CompilerParams(
            collective_id=0, has_side_effects=True, vmem_limit_bytes=58000000),
        name="step",
    )(
        charges, present_blocks, directions.reshape(4),
        wavefunction,
        left_operators.reshape(16, 256, 256),
        right_operators.reshape(16, 256, 256),
        rotations,
    )
    return sigma, regrouped


def solution(mesh):
    placed = (
        P("sec", None, None),
        P("op", "sec", None, None),
        P("op", "sec", None, None),
        P("sec", None, None),
        P("op"),
        P("op", "sec"),
        P("op", None),
    )
    return jax.shard_map(
        body,
        mesh=mesh,
        in_specs=placed,
        out_specs=(P("sec", "op", None), P("op", "sec", None, None)),
        check_vma=False,
    )
```

```python
import jax
import jax.numpy as jnp
from jax import lax
from jax.experimental import pallas as pl
from jax.experimental.pallas import tpu as pltpu
from jax.sharding import PartitionSpec as P

MESH = pl.DeviceIdType.MESH
F32 = jnp.float32
BF16 = jnp.bfloat16
NT = (((1,), (1,)), ((), ()))


def place(y, zh, x, c):
    return y * 16 + zh * 8 + x * 2 + c


def kernel(
    chg, pres, dirs, psi_h, left_h, right_h, rot_h,
    sig, reg,
    psi, left, right, rot, rot_t, rot_in, half, rotd, pay, hand,
    part, c_in, x_out, x_in, f2, y_out, y_in, z_out, z_in, e_out, e_in,
    in_sem, rot_s, rot_r, pay_s, pay_r, hand_s, hand_r, c_s, c_r, x_s, x_r, y_s, y_r, z_s, z_r, e_s, e_r,
):
    d = lax.axis_index("op")
    s = lax.axis_index("sec")
    y, zh, x, c = d // 16, (d // 8) % 2, (d // 2) % 4, d % 2
    core_peer = place(y, zh, x, 1 - c)
    x_peer = [place(y, zh, (x + o) % 4, c) for o in (1, 2, 3)]
    y_peer = [place((y + o) % 4, zh, x, c) for o in (1, 2, 3)]
    zh_peer = place(y, 1 - zh, x, c)
    up, down, across = (d + 1) % 64, (d + 63) % 64, (d + 32) % 64

    far_up = jnp.logical_and(x == 3, c == 1)
    far_down = jnp.logical_and(x == 0, c == 0)
    hand_up = jnp.logical_and(x == 2, c == 0)
    hand_down = jnp.logical_and(x == 1, c == 1)
    via_up = place((y + zh) % 4, zh, 2, 0)
    via_down = place((y + 3 + zh) % 4, zh, 1, 1)
    late_up = place(y, 1 - zh, 2, 0)
    late_down = place(y, 1 - zh, 1, 1)
    from_up = place((y + 4 - zh) % 4, zh, 3, 1)
    from_down = place((y + 1 - zh) % 4, zh, 0, 0)
    onto_up = place(y, 1 - zh, 0, 0)
    onto_down = place(y, 1 - zh, 3, 1)

    loads = [pltpu.make_async_copy(rot_h, rot, in_sem.at[0])]
    for p in range(4):
        i = (1, 2, 0, 3)[p]
        loads.append(pltpu.make_async_copy(left_h.at[:, i], left.at[i], in_sem.at[1 + p]))
    loads.append(pltpu.make_async_copy(psi_h, psi, in_sem.at[5]))
    loads.append(pltpu.make_async_copy(right_h, right, in_sem.at[6]))

    bar = pltpu.get_barrier_semaphore()
    for peer in [core_peer, zh_peer, up, down] + x_peer + y_peer:
        pl.semaphore_signal(bar, inc=1, device_id=(peer, s), device_id_type=MESH)

    @pl.when(s > 0)
    def _():
        for peer in (d, zh_peer):
            pl.semaphore_signal(bar, inc=1, device_id=(peer, s - 1), device_id_type=MESH)

    @pl.when(s < 3)
    def _():
        for peer in (d, zh_peer):
            pl.semaphore_signal(bar, inc=1, device_id=(peer, s + 1), device_id_type=MESH)

    def greet(when, peers):
        @pl.when(when)
        def _():
            for peer in peers:
                pl.semaphore_signal(bar, inc=1, device_id=(peer, s), device_id_type=MESH)

    greet(far_up, (via_up, late_down))
    greet(far_down, (via_down, late_up))
    greet(hand_up, (from_up, onto_up))
    greet(hand_down, (from_down, onto_down))

    for copy in loads:
        copy.start()
    loads[0].wait()
    half[16] = jnp.zeros((256, 256), BF16)

    def flip(i, _):
        rot_t[i + 1] = rot[i].T
        return 0

    lax.fori_loop(0, 4, flip, 0)
    rot_t[0] = jnp.zeros((256, 256), BF16)
    rot_t[5] = jnp.zeros((256, 256), BF16)
    reg[1] = jnp.zeros((4, 256, 256), BF16)

    def rotate(i):
        rows = left[i].reshape(1024, 256)
        rotd[pl.ds(4 * i, 4)] = jnp.dot(rows, rot[i], preferred_element_type=F32).astype(BF16).reshape(4, 256, 256)

    for i in (1, 2):
        loads[i].wait()
        rotate(i)

    kinds = [dirs[p] for p in range(4)]
    fresh = []
    for p in range(4):
        seen = jnp.int32(0)
        for q in range(p):
            seen = seen + (kinds[q] == kinds[p]).astype(jnp.int32)
        fresh.append((seen == 0).astype(jnp.int32))
    first = {}
    for k in (1, 2, 3):
        pick = jnp.int32(0)
        for p in range(1, 4):
            pick = pick + p * fresh[p] * (kinds[p] == k).astype(jnp.int32)
        first[k] = pick
    extra = 6 - first[1] - first[2] - first[3]
    extra = jnp.clip(extra, 0, 3)
    extra_kind = dirs[extra]

    def to_above():
        return pltpu.make_async_remote_copy(
            rot.at[3], rot_in.at[0], rot_s.at[0], rot_r.at[0], device_id=(d, s + 1), device_id_type=MESH)

    def to_below():
        return pltpu.make_async_remote_copy(
            rot.at[0], rot_in.at[1], rot_s.at[1], rot_r.at[1], device_id=(d, s - 1), device_id_type=MESH)

    def moved(k, j, i):
        to = {1: up, 2: down, 3: across}[k]
        n = 2 * (k - 1) + j
        return pltpu.make_async_remote_copy(
            pay.at[n, i], reg.at[2 * k + j, i], pay_s.at[n, i], pay_r.at[n, i],
            device_id=(to, s), device_id_type=MESH)

    def to_hand(k, j, i):
        n, h = 2 * (k - 1) + j, 2 * i + j
        return pltpu.make_async_remote_copy(
            pay.at[n, i], hand.at[h], pay_s.at[n, i], hand_r.at[h],
            device_id=({1: via_up, 2: via_down}[k], s), device_id_type=MESH)

    def from_hand(k, j, i):
        n, h = 2 * (k - 1) + j, 2 * i + j
        return pltpu.make_async_remote_copy(
            hand.at[h], reg.at[2 * k + j, i], hand_s.at[h], pay_r.at[n, i],
            device_id=({1: onto_up, 2: onto_down}[k], s), device_id_type=MESH)

    def send_far(sectors):
        for k, far in ((1, far_up), (2, far_down)):
            @pl.when(far)
            def _(k=k):
                for i in sectors:
                    for j in (0, 1):
                        (to_hand if i in (0, 1, 2) else moved)(k, j, i).start()

    def send_beside(sectors):
        for k, here in ((1, c == 0), (2, c == 1)):
            @pl.when(here)
            def _(k=k):
                for i in sectors:
                    for j in (0, 1):
                        moved(k, j, i).start()

    def send_ring(sectors):
        for k, here in ((1, (c == 1) & (x < 3)), (2, (c == 0) & (x > 0))):
            @pl.when(here)
            def _(k=k):
                for i in sectors:
                    for j in (0, 1):
                        moved(k, j, i).start()

    def send_across(sectors):
        for i in sectors:
            for j in (0, 1):
                moved(3, j, i).start()

    def hand_on(sectors):
        for k, here in ((1, hand_up), (2, hand_down)):
            @pl.when(here)
            def _(k=k):
                for i in sectors:
                    for j in (0, 1):
                        to_hand(k, j, i).wait_recv()
                        from_hand(k, j, i).start()

    def renormed(p, i):
        w = pres[p, i].astype(F32)
        return jnp.dot(rot_t[i + 1 + chg[p]], rotd[4 * i + p], preferred_element_type=F32) * w

    def firsts(k, i):
        pay[2 * (k - 1), i] = renormed(first[k], i).astype(BF16)

    def extras(i):
        block = renormed(extra, i)
        for k in (1, 2, 3):
            pay[2 * (k - 1) + 1, i] = (block * (extra_kind == k).astype(F32)).astype(BF16)
        reg[0, i] = (block * (extra_kind == 0).astype(F32)).astype(BF16)

    def all_of(i):
        for k in (1, 2, 3):
            firsts(k, i)
        extras(i)

    def inner(i, _):
        all_of(i)
        return 0

    lax.fori_loop(1, 3, inner, 0)
    sides = jnp.where(s > 0, 2, 0) + jnp.where(s < 3, 2, 0)
    corner = far_up | far_down | hand_up | hand_down
    pl.semaphore_wait(bar, 10 + sides + jnp.where(corner, 2, 0))

    @pl.when(s < 3)
    def _():
        to_above().start()

    @pl.when(s > 0)
    def _():
        to_below().start()

    send_far((1, 2))
    send_across((1, 2))
    send_beside((1, 2))

    loads[3].wait()
    loads[4].wait()
    loads[5].wait()

    def halve(i, _):
        both = jnp.dot(left[i].reshape(1024, 256), psi[i], preferred_element_type=F32).reshape(4, 256, 256)
        for p in range(4):
            half[4 * i + p] = (both[p] * pres[p, i].astype(F32)).astype(BF16)
        return 0

    lax.fori_loop(0, 4, halve, 0)

    loads[6].wait()
    row = lax.broadcasted_iota(jnp.int32, (256, 256), 0)
    col = lax.broadcasted_iota(jnp.int32, (256, 256), 1)
    natural = ((row // 8) % 4) * 64 + ((row // 4) % 2) * 32 + ((row // 32) % 4) * 8 + (row // 128) * 4 + row % 4
    order = (col == natural).astype(BF16)

    def target_sum(e, _):
        total = jnp.zeros((256, 256), F32)
        for p in range(4):
            src = e - 1 - chg[p]
            inside = jnp.logical_and(src >= 0, src <= 3)
            clipped = jnp.clip(src, 0, 3)
            lhs = half[jnp.where(inside, 4 * clipped + p, 16)]
            total = total + lax.dot_general(lhs, right[4 * p + clipped], NT, preferred_element_type=F32)
        placed = jnp.dot(order, total.astype(BF16), preferred_element_type=F32).astype(BF16)
        part[e, 0] = placed[:128]
        part[e, 1] = placed[128:]
        return 0

    def to_core(g):
        some = pl.ds(3 * g, 3)
        return pltpu.make_async_remote_copy(
            part.at[some, 1 - c], c_in.at[some], c_s.at[g], c_r.at[g], device_id=(core_peer, s), device_id_type=MESH)

    def to_x(g, o):
        some = pl.ds(3 * g, 3)
        return pltpu.make_async_remote_copy(
            x_out.at[some, (x + o + 1) % 4], x_in.at[o, some], x_s.at[g, o], x_r.at[g, o],
            device_id=(x_peer[o], s), device_id_type=MESH)

    for g in (0, 1):
        lax.fori_loop(3 * g, 3 * g + 3, target_sum, 0)
        to_core(g).start()

    for i in (0, 3):
        rotate(i)

    @pl.when(s > 0)
    def _():
        to_above().wait_recv()
        rot_t[0] = rot_in[0].T

    @pl.when(s < 3)
    def _():
        to_below().wait_recv()
        rot_t[5] = rot_in[1].T

    def outer(q, _):
        all_of(3 * q)
        return 0

    lax.fori_loop(0, 2, outer, 0)
    send_far((0, 3))
    send_across((0,))
    def core_sum(e, _):
        both = part[e, c].astype(F32) + c_in[e].astype(F32)
        x_out[e] = both.reshape(4, 32, 256).astype(BF16)
        return 0

    for g in (0, 1):
        to_core(g).wait_recv()
        lax.fori_loop(3 * g, 3 * g + 3, core_sum, 0)
        for o in range(3):
            to_x(g, o).start()
    hand_on((1, 2))
    send_beside((0, 3))
    send_ring((0, 1, 2, 3))
    for g in (0, 1):
        for o in range(3):
            to_x(g, o).wait_recv()
    rows = pl.ds(pl.multiple_of(x * 32, 32), 32)

    def x_sum(e, _):
        total = part[e, c, rows].astype(F32) + c_in[e, rows].astype(F32)
        for o in range(3):
            total = total + x_in[o, e].astype(F32)
        for q in range(4):
            f2[q, e] = total[8 * q:8 * q + 8]
        return 0

    lax.fori_loop(0, 6, x_sum, 0)
    for q in range(4):
        y_out[q] = f2[q].reshape(48, 256).astype(BF16)
    to_y = []
    for o in range(3):
        copy = pltpu.make_async_remote_copy(
            y_out.at[(y + o + 1) % 4], y_in.at[o], y_s.at[o], y_r.at[o],
            device_id=(y_peer[o], s), device_id_type=MESH)
        copy.start()
        to_y.append(copy)
    send_across((3,))
    hand_on((0,))
    for copy in to_y:
        copy.wait_recv()
    total = f2[y].reshape(48, 256)
    for o in range(3):
        total = total + y_in[o].astype(F32)
    z_out[...] = total[8:40].astype(BF16)
    e_out[0] = total[0:8]
    e_out[1] = total[40:48]
    to_z = pltpu.make_async_remote_copy(
        z_out, z_in, z_s.at[0], z_r.at[0], device_id=(zh_peer, s), device_id_type=MESH)
    to_z.start()

    def edge(side, far):
        op_to = zh_peer if far else d
        sec_to = s + 1 if side else s - 1
        return pltpu.make_async_remote_copy(
            e_out.at[side], e_in.at[side, far], e_s.at[side, far], e_r.at[side, far],
            device_id=(op_to, sec_to), device_id_type=MESH)

    @pl.when(s < 3)
    def _():
        edge(1, 0).start()
        edge(1, 1).start()

    @pl.when(s > 0)
    def _():
        edge(0, 0).start()
        edge(0, 1).start()

    to_z.wait_recv()
    mine = (total[8:40] + z_in[...].astype(F32)).reshape(4, 8, 256)
    f2[0, pl.ds(0, 4)] = mine

    @pl.when(s > 0)
    def _():
        edge(1, 0).wait_recv()
        edge(1, 1).wait_recv()
        f2[0, 0] = f2[0, 0] + e_in[1, 0] + e_in[1, 1]

    @pl.when(s < 3)
    def _():
        edge(0, 0).wait_recv()
        edge(0, 1).wait_recv()
        f2[0, 3] = f2[0, 3] + e_in[0, 0] + e_in[0, 1]

    final = f2[0, pl.ds(0, 4)] * (1.0 / 16.0)
    sig[...] = jnp.where(zh == 0, final[:, 0:4], final[:, 4:8])

    for copy in [to_z] + to_y:
        copy.wait_send()
    for g in (0, 1):
        to_core(g).wait_send()
        for o in range(3):
            to_x(g, o).wait_send()

    @pl.when(s < 3)
    def _():
        edge(1, 0).wait_send()
        edge(1, 1).wait_send()
        to_above().wait_send()

    @pl.when(s > 0)
    def _():
        edge(0, 0).wait_send()
        edge(0, 1).wait_send()
        to_below().wait_send()

    for k, here in ((1, hand_up), (2, hand_down)):
        @pl.when(here)
        def _(k=k):
            for j in (0, 1):
                for i in (0, 1, 2):
                    from_hand(k, j, i).wait_send()

    for k in (1, 2, 3):
        for j in (0, 1):
            for i in range(4):
                moved(k, j, i).wait()


def body(wavefunction, left_operators, right_operators, rotations, charges, present_blocks, directions):
    hbm = pl.BlockSpec(memory_space=pltpu.HBM)
    vmem = pl.BlockSpec(memory_space=pltpu.VMEM)
    smem = pl.BlockSpec(memory_space=pltpu.SMEM)
    dma = pltpu.SemaphoreType.DMA
    sigma, regrouped = pl.pallas_call(
        kernel,
        out_shape=(
            pltpu.VMEM((4, 4, 256), F32),
            pltpu.VMEM((8, 4, 256, 256), BF16),
        ),
        in_specs=[smem, smem, smem, hbm, hbm, hbm, hbm],
        out_specs=(vmem, vmem),
        scratch_shapes=[
            pltpu.VMEM((4, 256, 256), BF16),
            pltpu.VMEM((4, 4, 256, 256), BF16),
            pltpu.VMEM((16, 256, 256), BF16),
            pltpu.VMEM((4, 256, 256), BF16),
            pltpu.VMEM((6, 256, 256), BF16),
            pltpu.VMEM((2, 256, 256), BF16),
            pltpu.VMEM((17, 256, 256), BF16),
            pltpu.VMEM((16, 256, 256), BF16),
            pltpu.VMEM((6, 4, 256, 256), BF16),
            pltpu.VMEM((6, 256, 256), BF16),
            pltpu.VMEM((6, 2, 128, 256), BF16),
            pltpu.VMEM((6, 128, 256), BF16),
            pltpu.VMEM((6, 4, 32, 256), BF16),
            pltpu.VMEM((3, 6, 32, 256), BF16),
            pltpu.VMEM((4, 6, 8, 256), F32),
            pltpu.VMEM((4, 48, 256), BF16),
            pltpu.VMEM((3, 48, 256), BF16),
            pltpu.VMEM((32, 256), BF16),
            pltpu.VMEM((32, 256), BF16),
            pltpu.VMEM((2, 8, 256), F32),
            pltpu.VMEM((2, 2, 8, 256), F32),
            dma((7,)), dma((2,)), dma((2,)), dma((6, 4)), dma((6, 4)), dma((6,)), dma((6,)),
            dma((2,)), dma((2,)), dma((2, 3)), dma((2, 3)), dma((3,)), dma((3,)),
            dma((1,)), dma((1,)), dma((2, 2)), dma((2, 2)),
        ],
        compiler_params=pltpu.CompilerParams(
            collective_id=0, has_side_effects=True, vmem_limit_bytes=58000000),
        name="step",
    )(
        charges, present_blocks, directions.reshape(4),
        wavefunction,
        left_operators,
        right_operators.reshape(16, 256, 256),
        rotations,
    )
    return sigma, regrouped


def solution(mesh):
    placed = (
        P("sec", None, None),
        P("op", "sec", None, None),
        P("op", "sec", None, None),
        P("sec", None, None),
        P("op"),
        P("op", "sec"),
        P("op", None),
    )
    return jax.shard_map(
        body,
        mesh=mesh,
        in_specs=placed,
        out_specs=(P("sec", "op", None), P("op", "sec", None, None)),
        check_vma=False,
    )
```

```python
import jax
import jax.numpy as jnp
from jax import lax
from jax.experimental import pallas as pl
from jax.experimental.pallas import tpu as pltpu
from jax.sharding import PartitionSpec as P

MESH = pl.DeviceIdType.MESH
F32 = jnp.float32
BF16 = jnp.bfloat16
NT = (((1,), (1,)), ((), ()))
MIDDLE = [(1, 0), (1, 1), (2, 0), (2, 1), (3, 0)]
SIDE = [(0, 0), (0, 1)]


def place(y, zh, x, c):
    return y * 16 + zh * 8 + x * 2 + c


def kernel(
    chg, pres, dirs, psi_h, left_h, right_h, rot_h,
    sig, reg,
    psi, left, right, rot, rot_t, rot_in, half, rotd, pay, hand,
    part, c_in, x_out, x_in, f2, y_out, y_in, z_out, z_in, e_out, e_in,
    in_sem, rot_s, rot_r, pay_s, pay_r, hand_s, hand_r, c_s, c_r, x_s, x_r, y_s, y_r, z_s, z_r, e_s, e_r,
):
    d = lax.axis_index("op")
    s = lax.axis_index("sec")
    y, zh, x, c = d // 16, (d // 8) % 2, (d // 2) % 4, d % 2
    core_peer = place(y, zh, x, 1 - c)
    x_peer = [place(y, zh, (x + o) % 4, c) for o in (1, 2, 3)]
    y_peer = [place((y + o) % 4, zh, x, c) for o in (1, 2, 3)]
    zh_peer = place(y, 1 - zh, x, c)
    up, down, across = (d + 1) % 64, (d + 63) % 64, (d + 32) % 64

    far_up = jnp.logical_and(x == 3, c == 1)
    far_down = jnp.logical_and(x == 0, c == 0)
    hand_up = jnp.logical_and(x == 2, c == 0)
    hand_down = jnp.logical_and(x == 1, c == 1)
    via_up = place((y + zh) % 4, zh, 2, 0)
    via_down = place((y + 3 + zh) % 4, zh, 1, 1)
    side_up = (x == 3) & (c == 0)
    side_down = (x == 0) & (c == 1)
    past_up = place((y + zh) % 4, zh, 3, 0)
    past_down = place((y + 3 + zh) % 4, zh, 0, 1)
    late_up = place(y, 1 - zh, 2, 0)
    late_down = place(y, 1 - zh, 1, 1)
    from_up = place((y + 4 - zh) % 4, zh, 3, 1)
    from_down = place((y + 1 - zh) % 4, zh, 0, 0)
    onto_up = place(y, 1 - zh, 0, 0)
    onto_down = place(y, 1 - zh, 3, 1)

    loads = [pltpu.make_async_copy(rot_h, rot, in_sem.at[0])]
    for p in range(4):
        i = (1, 2, 0, 3)[p]
        loads.append(pltpu.make_async_copy(left_h.at[:, i], left.at[i], in_sem.at[1 + p]))
    loads.append(pltpu.make_async_copy(psi_h, psi, in_sem.at[5]))
    loads.append(pltpu.make_async_copy(right_h, right, in_sem.at[6]))

    bar = pltpu.get_barrier_semaphore()
    for peer in [core_peer, zh_peer, up, down] + x_peer + y_peer:
        pl.semaphore_signal(bar, inc=1, device_id=(peer, s), device_id_type=MESH)

    @pl.when(s > 0)
    def _():
        for peer in (d, zh_peer):
            pl.semaphore_signal(bar, inc=1, device_id=(peer, s - 1), device_id_type=MESH)

    @pl.when(s < 3)
    def _():
        for peer in (d, zh_peer):
            pl.semaphore_signal(bar, inc=1, device_id=(peer, s + 1), device_id_type=MESH)

    def greet(when, peers):
        @pl.when(when)
        def _():
            for peer in peers:
                pl.semaphore_signal(bar, inc=1, device_id=(peer, s), device_id_type=MESH)

    greet(far_up, (via_up, late_down, past_up, place(y, 1 - zh, 0, 1)))
    greet(far_down, (via_down, late_up, past_down, place(y, 1 - zh, 3, 0)))
    greet(side_up, (from_up, onto_up))
    greet(side_down, (from_down, onto_down))
    greet(hand_up, (from_up, onto_up))
    greet(hand_down, (from_down, onto_down))

    for copy in loads:
        copy.start()
    loads[0].wait()
    half[16] = jnp.zeros((256, 256), BF16)

    def flip(i, _):
        rot_t[i + 1] = rot[i].T
        return 0

    lax.fori_loop(0, 4, flip, 0)
    rot_t[0] = jnp.zeros((256, 256), BF16)
    rot_t[5] = jnp.zeros((256, 256), BF16)
    reg[1] = jnp.zeros((4, 256, 256), BF16)

    def rotate(i):
        rows = left[i].reshape(1024, 256)
        rotd[pl.ds(4 * i, 4)] = jnp.dot(rows, rot[i], preferred_element_type=F32).astype(BF16).reshape(4, 256, 256)

    for i in (1, 2):
        loads[i].wait()
        rotate(i)

    kinds = [dirs[p] for p in range(4)]
    fresh = []
    for p in range(4):
        seen = jnp.int32(0)
        for q in range(p):
            seen = seen + (kinds[q] == kinds[p]).astype(jnp.int32)
        fresh.append((seen == 0).astype(jnp.int32))
    first = {}
    for k in (1, 2, 3):
        pick = jnp.int32(0)
        for p in range(1, 4):
            pick = pick + p * fresh[p] * (kinds[p] == k).astype(jnp.int32)
        first[k] = pick
    extra = 6 - first[1] - first[2] - first[3]
    extra = jnp.clip(extra, 0, 3)
    extra_kind = dirs[extra]

    def to_above():
        return pltpu.make_async_remote_copy(
            rot.at[3], rot_in.at[0], rot_s.at[0], rot_r.at[0], device_id=(d, s + 1), device_id_type=MESH)

    def to_below():
        return pltpu.make_async_remote_copy(
            rot.at[0], rot_in.at[1], rot_s.at[1], rot_r.at[1], device_id=(d, s - 1), device_id_type=MESH)

    def moved(k, j, i):
        to = {1: up, 2: down, 3: across}[k]
        n = 2 * (k - 1) + j
        return pltpu.make_async_remote_copy(
            pay.at[n, i], reg.at[2 * k + j, i], pay_s.at[n, i], pay_r.at[n, i],
            device_id=(to, s), device_id_type=MESH)

    def to_hand(k, j, i):
        n, h = 2 * (k - 1) + j, 2 * i + j
        return pltpu.make_async_remote_copy(
            pay.at[n, i], hand.at[h], pay_s.at[n, i], hand_r.at[h],
            device_id=((
                {1: past_up, 2: past_down} if (i, j) in SIDE else {1: via_up, 2: via_down})[k], s), device_id_type=MESH)

    def from_hand(k, j, i):
        n, h = 2 * (k - 1) + j, 2 * i + j
        return pltpu.make_async_remote_copy(
            hand.at[h], reg.at[2 * k + j, i], hand_s.at[h], pay_r.at[n, i],
            device_id=({1: onto_up, 2: onto_down}[k], s), device_id_type=MESH)

    def send_far(sectors):
        for k, far in ((1, far_up), (2, far_down)):
            @pl.when(far)
            def _(k=k):
                for i in sectors:
                    for j in (0, 1):
                        (to_hand if (i, j) in SIDE + MIDDLE else moved)(k, j, i).start()

    def send_beside(sectors):
        for k, here in ((1, c == 0), (2, c == 1)):
            @pl.when(here)
            def _(k=k):
                for i in sectors:
                    for j in (0, 1):
                        moved(k, j, i).start()

    def send_ring(sectors):
        for k, here in ((1, (c == 1) & (x < 3)), (2, (c == 0) & (x > 0))):
            @pl.when(here)
            def _(k=k):
                for i in sectors:
                    for j in (0, 1):
                        moved(k, j, i).start()

    def send_across(sectors):
        for i in sectors:
            for j in (0, 1):
                moved(3, j, i).start()

    def hand_on(blocks, ups, downs):
        for k, here in ((1, ups), (2, downs)):
            @pl.when(here)
            def _(k=k):
                for i, j in blocks:
                    to_hand(k, j, i).wait_recv()
                    from_hand(k, j, i).start()

    def renormed(p, i):
        w = pres[p, i].astype(F32)
        return jnp.dot(rot_t[i + 1 + chg[p]], rotd[4 * i + p], preferred_element_type=F32) * w

    def firsts(k, i):
        pay[2 * (k - 1), i] = renormed(first[k], i).astype(BF16)

    def extras(i):
        block = renormed(extra, i)
        for k in (1, 2, 3):
            pay[2 * (k - 1) + 1, i] = (block * (extra_kind == k).astype(F32)).astype(BF16)
        reg[0, i] = (block * (extra_kind == 0).astype(F32)).astype(BF16)

    def all_of(i):
        for k in (1, 2, 3):
            firsts(k, i)
        extras(i)

    def inner(i, _):
        all_of(i)
        return 0

    lax.fori_loop(1, 3, inner, 0)
    sides = jnp.where(s > 0, 2, 0) + jnp.where(s < 3, 2, 0)
    far = far_up | far_down
    helps = hand_up | hand_down | side_up | side_down
    pl.semaphore_wait(bar, 10 + sides + jnp.where(far, 4, 0) + jnp.where(helps, 2, 0))

    @pl.when(s < 3)
    def _():
        to_above().start()

    @pl.when(s > 0)
    def _():
        to_below().start()

    send_far((1, 2))
    send_across((1, 2))
    send_beside((1, 2))

    loads[3].wait()
    loads[4].wait()
    loads[5].wait()

    def halve(i, _):
        both = jnp.dot(left[i].reshape(1024, 256), psi[i], preferred_element_type=F32).reshape(4, 256, 256)
        for p in range(4):
            half[4 * i + p] = (both[p] * pres[p, i].astype(F32)).astype(BF16)
        return 0

    lax.fori_loop(0, 4, halve, 0)

    loads[6].wait()
    row = lax.broadcasted_iota(jnp.int32, (256, 256), 0)
    col = lax.broadcasted_iota(jnp.int32, (256, 256), 1)
    natural = ((row // 8) % 4) * 64 + ((row // 4) % 2) * 32 + ((row // 32) % 4) * 8 + (row // 128) * 4 + row % 4
    order = (col == natural).astype(BF16)

    def target_sum(e, _):
        total = jnp.zeros((256, 256), F32)
        for p in range(4):
            src = e - 1 - chg[p]
            inside = jnp.logical_and(src >= 0, src <= 3)
            clipped = jnp.clip(src, 0, 3)
            lhs = half[jnp.where(inside, 4 * clipped + p, 16)]
            total = total + lax.dot_general(lhs, right[4 * p + clipped], NT, preferred_element_type=F32)
        placed = jnp.dot(order, total.astype(BF16), preferred_element_type=F32).astype(BF16)
        part[e, 0] = placed[:128]
        part[e, 1] = placed[128:]
        return 0

    def to_core(g):
        some = pl.ds(3 * g, 3)
        return pltpu.make_async_remote_copy(
            part.at[some, 1 - c], c_in.at[some], c_s.at[g], c_r.at[g], device_id=(core_peer, s), device_id_type=MESH)

    def to_x(g, o):
        some = pl.ds(3 * g, 3)
        return pltpu.make_async_remote_copy(
            x_out.at[some, (x + o + 1) % 4], x_in.at[o, some], x_s.at[g, o], x_r.at[g, o],
            device_id=(x_peer[o], s), device_id_type=MESH)

    for g in (0, 1):
        lax.fori_loop(3 * g, 3 * g + 3, target_sum, 0)
        to_core(g).start()

    for i in (0, 3):
        rotate(i)

    @pl.when(s > 0)
    def _():
        to_above().wait_recv()
        rot_t[0] = rot_in[0].T

    @pl.when(s < 3)
    def _():
        to_below().wait_recv()
        rot_t[5] = rot_in[1].T

    def outer(q, _):
        all_of(3 * q)
        return 0

    lax.fori_loop(0, 2, outer, 0)
    send_far((0, 3))
    send_across((0,))
    def core_sum(e, _):
        both = part[e, c].astype(F32) + c_in[e].astype(F32)
        x_out[e] = both.reshape(4, 32, 256).astype(BF16)
        return 0

    for g in (0, 1):
        to_core(g).wait_recv()
        lax.fori_loop(3 * g, 3 * g + 3, core_sum, 0)
        for o in range(3):
            to_x(g, o).start()
    hand_on([b for b in MIDDLE if b[0] in (1, 2)], hand_up, hand_down)
    send_beside((0, 3))
    send_ring((0, 1, 2, 3))
    for g in (0, 1):
        for o in range(3):
            to_x(g, o).wait_recv()
    rows = pl.ds(pl.multiple_of(x * 32, 32), 32)

    def x_sum(e, _):
        total = part[e, c, rows].astype(F32) + c_in[e, rows].astype(F32)
        for o in range(3):
            total = total + x_in[o, e].astype(F32)
        for q in range(4):
            f2[q, e] = total[8 * q:8 * q + 8]
        return 0

    lax.fori_loop(0, 6, x_sum, 0)
    for q in range(4):
        y_out[q] = f2[q].reshape(48, 256).astype(BF16)
    to_y = []
    for o in range(3):
        copy = pltpu.make_async_remote_copy(
            y_out.at[(y + o + 1) % 4], y_in.at[o], y_s.at[o], y_r.at[o],
            device_id=(y_peer[o], s), device_id_type=MESH)
        copy.start()
        to_y.append(copy)
    send_across((3,))
    hand_on(SIDE, side_up, side_down)
    hand_on([b for b in MIDDLE if b[0] in (0, 3)], hand_up, hand_down)
    for copy in to_y:
        copy.wait_recv()
    total = f2[y].reshape(48, 256)
    for o in range(3):
        total = total + y_in[o].astype(F32)
    z_out[...] = total[8:40].astype(BF16)
    e_out[0] = total[0:8]
    e_out[1] = total[40:48]
    to_z = pltpu.make_async_remote_copy(
        z_out, z_in, z_s.at[0], z_r.at[0], device_id=(zh_peer, s), device_id_type=MESH)
    to_z.start()

    def edge(side, far):
        op_to = zh_peer if far else d
        sec_to = s + 1 if side else s - 1
        return pltpu.make_async_remote_copy(
            e_out.at[side], e_in.at[side, far], e_s.at[side, far], e_r.at[side, far],
            device_id=(op_to, sec_to), device_id_type=MESH)

    @pl.when(s < 3)
    def _():
        edge(1, 0).start()
        edge(1, 1).start()

    @pl.when(s > 0)
    def _():
        edge(0, 0).start()
        edge(0, 1).start()

    to_z.wait_recv()
    mine = (total[8:40] + z_in[...].astype(F32)).reshape(4, 8, 256)
    f2[0, pl.ds(0, 4)] = mine

    @pl.when(s > 0)
    def _():
        edge(1, 0).wait_recv()
        edge(1, 1).wait_recv()
        f2[0, 0] = f2[0, 0] + e_in[1, 0] + e_in[1, 1]

    @pl.when(s < 3)
    def _():
        edge(0, 0).wait_recv()
        edge(0, 1).wait_recv()
        f2[0, 3] = f2[0, 3] + e_in[0, 0] + e_in[0, 1]

    final = f2[0, pl.ds(0, 4)] * (1.0 / 16.0)
    sig[...] = jnp.where(zh == 0, final[:, 0:4], final[:, 4:8])

    for copy in [to_z] + to_y:
        copy.wait_send()
    for g in (0, 1):
        to_core(g).wait_send()
        for o in range(3):
            to_x(g, o).wait_send()

    @pl.when(s < 3)
    def _():
        edge(1, 0).wait_send()
        edge(1, 1).wait_send()
        to_above().wait_send()

    @pl.when(s > 0)
    def _():
        edge(0, 0).wait_send()
        edge(0, 1).wait_send()
        to_below().wait_send()

    for k, here, blocks in (
        (1, hand_up, MIDDLE), (2, hand_down, MIDDLE), (1, side_up, SIDE), (2, side_down, SIDE),
    ):
        @pl.when(here)
        def _(k=k, blocks=blocks):
            for i, j in blocks:
                from_hand(k, j, i).wait_send()

    for k in (1, 2, 3):
        for j in (0, 1):
            for i in range(4):
                moved(k, j, i).wait()


def body(wavefunction, left_operators, right_operators, rotations, charges, present_blocks, directions):
    hbm = pl.BlockSpec(memory_space=pltpu.HBM)
    vmem = pl.BlockSpec(memory_space=pltpu.VMEM)
    smem = pl.BlockSpec(memory_space=pltpu.SMEM)
    dma = pltpu.SemaphoreType.DMA
    sigma, regrouped = pl.pallas_call(
        kernel,
        out_shape=(
            pltpu.VMEM((4, 4, 256), F32),
            pltpu.VMEM((8, 4, 256, 256), BF16),
        ),
        in_specs=[smem, smem, smem, hbm, hbm, hbm, hbm],
        out_specs=(vmem, vmem),
        scratch_shapes=[
            pltpu.VMEM((4, 256, 256), BF16),
            pltpu.VMEM((4, 4, 256, 256), BF16),
            pltpu.VMEM((16, 256, 256), BF16),
            pltpu.VMEM((4, 256, 256), BF16),
            pltpu.VMEM((6, 256, 256), BF16),
            pltpu.VMEM((2, 256, 256), BF16),
            pltpu.VMEM((17, 256, 256), BF16),
            pltpu.VMEM((16, 256, 256), BF16),
            pltpu.VMEM((6, 4, 256, 256), BF16),
            pltpu.VMEM((8, 256, 256), BF16),
            pltpu.VMEM((6, 2, 128, 256), BF16),
            pltpu.VMEM((6, 128, 256), BF16),
            pltpu.VMEM((6, 4, 32, 256), BF16),
            pltpu.VMEM((3, 6, 32, 256), BF16),
            pltpu.VMEM((4, 6, 8, 256), F32),
            pltpu.VMEM((4, 48, 256), BF16),
            pltpu.VMEM((3, 48, 256), BF16),
            pltpu.VMEM((32, 256), BF16),
            pltpu.VMEM((32, 256), BF16),
            pltpu.VMEM((2, 8, 256), F32),
            pltpu.VMEM((2, 2, 8, 256), F32),
            dma((7,)), dma((2,)), dma((2,)), dma((6, 4)), dma((6, 4)), dma((8,)), dma((8,)),
            dma((2,)), dma((2,)), dma((2, 3)), dma((2, 3)), dma((3,)), dma((3,)),
            dma((1,)), dma((1,)), dma((2, 2)), dma((2, 2)),
        ],
        compiler_params=pltpu.CompilerParams(
            collective_id=0, has_side_effects=True, vmem_limit_bytes=58000000),
        name="step",
    )(
        charges, present_blocks, directions.reshape(4),
        wavefunction,
        left_operators,
        right_operators.reshape(16, 256, 256),
        rotations,
    )
    return sigma, regrouped


def solution(mesh):
    placed = (
        P("sec", None, None),
        P("op", "sec", None, None),
        P("op", "sec", None, None),
        P("sec", None, None),
        P("op"),
        P("op", "sec"),
        P("op", None),
    )
    return jax.shard_map(
        body,
        mesh=mesh,
        in_specs=placed,
        out_specs=(P("sec", "op", None), P("op", "sec", None, None)),
        check_vma=False,
    )
```

```python
import jax
import jax.numpy as jnp
from jax import lax
from jax.experimental import pallas as pl
from jax.experimental.pallas import tpu as pltpu
from jax.sharding import PartitionSpec as P

MESH = pl.DeviceIdType.MESH
F32 = jnp.float32
BF16 = jnp.bfloat16
NT = (((1,), (1,)), ((), ()))
MIDDLE = [(1, 0), (1, 1), (2, 0), (2, 1), (3, 0)]
SIDE = [(0, 0), (0, 1)]


def place(y, zh, x, c):
    return y * 16 + zh * 8 + x * 2 + c


def kernel(
    chg, pres, dirs, psi_h, left_h, right_h, rot_h,
    sig, reg,
    psi, left, right, rot, rot_t, rot_in, half, rotd, pay, hand,
    part, c_in, x_out, x_in, f2, y_out, y_in, z_out, z_in, e_out, e_in,
    in_sem, rot_s, rot_r, pay_s, pay_r, hand_s, hand_r, c_s, c_r, x_s, x_r, y_s, y_r, z_s, z_r, e_s, e_r,
):
    d = lax.axis_index("op")
    s = lax.axis_index("sec")
    y, zh, x, c = d // 16, (d // 8) % 2, (d // 2) % 4, d % 2
    core_peer = place(y, zh, x, 1 - c)
    x_peer = [place(y, zh, (x + o) % 4, c) for o in (1, 2, 3)]
    y_peer = [place((y + o) % 4, zh, x, c) for o in (1, 2, 3)]
    zh_peer = place(y, 1 - zh, x, c)
    up, down, across = (d + 1) % 64, (d + 63) % 64, (d + 32) % 64

    far_up = jnp.logical_and(x == 3, c == 1)
    far_down = jnp.logical_and(x == 0, c == 0)
    hand_up = jnp.logical_and(x == 2, c == 0)
    hand_down = jnp.logical_and(x == 1, c == 1)
    via_up = place((y + zh) % 4, zh, 2, 0)
    via_down = place((y + 3 + zh) % 4, zh, 1, 1)
    side_up = (x == 3) & (c == 0)
    side_down = (x == 0) & (c == 1)
    past_up = place((y + zh) % 4, zh, 3, 0)
    past_down = place((y + 3 + zh) % 4, zh, 0, 1)
    late_up = place(y, 1 - zh, 2, 0)
    late_down = place(y, 1 - zh, 1, 1)
    from_up = place((y + 4 - zh) % 4, zh, 3, 1)
    from_down = place((y + 1 - zh) % 4, zh, 0, 0)
    onto_up = place(y, 1 - zh, 0, 0)
    onto_down = place(y, 1 - zh, 3, 1)

    loads = [pltpu.make_async_copy(rot_h, rot, in_sem.at[0])]
    for p in range(4):
        i = (1, 2, 0, 3)[p]
        loads.append(pltpu.make_async_copy(left_h.at[:, i], left.at[i], in_sem.at[1 + p]))
    loads.append(pltpu.make_async_copy(psi_h, psi, in_sem.at[5]))
    loads.append(pltpu.make_async_copy(right_h, right, in_sem.at[6]))

    bar = pltpu.get_barrier_semaphore()
    for peer in [core_peer, zh_peer, up, down] + x_peer + y_peer:
        pl.semaphore_signal(bar, inc=1, device_id=(peer, s), device_id_type=MESH)

    @pl.when(s > 0)
    def _():
        for peer in (d, zh_peer):
            pl.semaphore_signal(bar, inc=1, device_id=(peer, s - 1), device_id_type=MESH)

    @pl.when(s < 3)
    def _():
        for peer in (d, zh_peer):
            pl.semaphore_signal(bar, inc=1, device_id=(peer, s + 1), device_id_type=MESH)

    def greet(when, peers):
        @pl.when(when)
        def _():
            for peer in peers:
                pl.semaphore_signal(bar, inc=1, device_id=(peer, s), device_id_type=MESH)

    greet(far_up, (via_up, late_down, past_up, place(y, 1 - zh, 0, 1)))
    greet(far_down, (via_down, late_up, past_down, place(y, 1 - zh, 3, 0)))
    greet(side_up, (from_up, onto_up))
    greet(side_down, (from_down, onto_down))
    greet(hand_up, (from_up, onto_up))
    greet(hand_down, (from_down, onto_down))

    for copy in loads:
        copy.start()
    loads[0].wait()
    half[16] = jnp.zeros((256, 256), BF16)

    def flip(i, _):
        rot_t[i + 1] = rot[i].T
        return 0

    lax.fori_loop(0, 4, flip, 0)
    rot_t[0] = jnp.zeros((256, 256), BF16)
    rot_t[5] = jnp.zeros((256, 256), BF16)
    reg[1] = jnp.zeros((4, 256, 256), BF16)

    def rotate(i):
        rows = left[i].reshape(1024, 256)
        rotd[pl.ds(4 * i, 4)] = jnp.dot(rows, rot[i], preferred_element_type=F32).astype(BF16).reshape(4, 256, 256)

    for i in (1, 2):
        loads[i].wait()
        rotate(i)

    kinds = [dirs[p] for p in range(4)]
    fresh = []
    for p in range(4):
        seen = jnp.int32(0)
        for q in range(p):
            seen = seen + (kinds[q] == kinds[p]).astype(jnp.int32)
        fresh.append((seen == 0).astype(jnp.int32))
    first = {}
    for k in (1, 2, 3):
        pick = jnp.int32(0)
        for p in range(1, 4):
            pick = pick + p * fresh[p] * (kinds[p] == k).astype(jnp.int32)
        first[k] = pick
    extra = 6 - first[1] - first[2] - first[3]
    extra = jnp.clip(extra, 0, 3)
    extra_kind = dirs[extra]

    def to_above():
        return pltpu.make_async_remote_copy(
            rot.at[3], rot_in.at[0], rot_s.at[0], rot_r.at[0], device_id=(d, s + 1), device_id_type=MESH)

    def to_below():
        return pltpu.make_async_remote_copy(
            rot.at[0], rot_in.at[1], rot_s.at[1], rot_r.at[1], device_id=(d, s - 1), device_id_type=MESH)

    def moved(k, j, i):
        to = {1: up, 2: down, 3: across}[k]
        n = 2 * (k - 1) + j
        return pltpu.make_async_remote_copy(
            pay.at[n, i], reg.at[2 * k + j, i], pay_s.at[n, i], pay_r.at[n, i],
            device_id=(to, s), device_id_type=MESH)

    def to_hand(k, j, i):
        n, h = 2 * (k - 1) + j, 2 * i + j
        return pltpu.make_async_remote_copy(
            pay.at[n, i], hand.at[h], pay_s.at[n, i], hand_r.at[h],
            device_id=((
                {1: past_up, 2: past_down} if (i, j) in SIDE else {1: via_up, 2: via_down})[k], s), device_id_type=MESH)

    def from_hand(k, j, i):
        n, h = 2 * (k - 1) + j, 2 * i + j
        return pltpu.make_async_remote_copy(
            hand.at[h], reg.at[2 * k + j, i], hand_s.at[h], pay_r.at[n, i],
            device_id=({1: onto_up, 2: onto_down}[k], s), device_id_type=MESH)

    def send_far(sectors):
        for k, far in ((1, far_up), (2, far_down)):
            @pl.when(far)
            def _(k=k):
                for i in sectors:
                    for j in (0, 1):
                        (to_hand if (i, j) in SIDE + MIDDLE else moved)(k, j, i).start()

    def send_beside(sectors):
        for k, here in ((1, c == 0), (2, c == 1)):
            @pl.when(here)
            def _(k=k):
                for i in sectors:
                    for j in (0, 1):
                        moved(k, j, i).start()

    def send_ring(sectors):
        for k, here in ((1, (c == 1) & (x < 3)), (2, (c == 0) & (x > 0))):
            @pl.when(here)
            def _(k=k):
                for i in sectors:
                    for j in (0, 1):
                        moved(k, j, i).start()

    def send_across(sectors):
        for i in sectors:
            for j in (0, 1):
                moved(3, j, i).start()

    def hand_on(blocks, ups, downs):
        for k, here in ((1, ups), (2, downs)):
            @pl.when(here)
            def _(k=k):
                for i, j in blocks:
                    to_hand(k, j, i).wait_recv()
                    from_hand(k, j, i).start()

    def renormed(p, i):
        w = pres[p, i].astype(F32)
        return jnp.dot(rot_t[i + 1 + chg[p]], rotd[4 * i + p], preferred_element_type=F32) * w

    def firsts(k, i):
        pay[2 * (k - 1), i] = renormed(first[k], i).astype(BF16)

    def extras(i):
        block = renormed(extra, i)
        for k in (1, 2, 3):
            pay[2 * (k - 1) + 1, i] = (block * (extra_kind == k).astype(F32)).astype(BF16)
        reg[0, i] = (block * (extra_kind == 0).astype(F32)).astype(BF16)

    def all_of(i):
        for k in (1, 2, 3):
            firsts(k, i)
        extras(i)

    def inner(i, _):
        all_of(i)
        return 0

    lax.fori_loop(1, 3, inner, 0)
    sides = jnp.where(s > 0, 2, 0) + jnp.where(s < 3, 2, 0)
    far = far_up | far_down
    helps = hand_up | hand_down | side_up | side_down
    pl.semaphore_wait(bar, 10 + sides + jnp.where(far, 4, 0) + jnp.where(helps, 2, 0))

    @pl.when(s < 3)
    def _():
        to_above().start()

    @pl.when(s > 0)
    def _():
        to_below().start()

    send_far((1, 2))
    send_across((1, 2))
    send_beside((1, 2))

    loads[3].wait()
    loads[4].wait()
    loads[5].wait()

    def halve(i, _):
        both = jnp.dot(left[i].reshape(1024, 256), psi[i], preferred_element_type=F32).reshape(4, 256, 256)
        for p in range(4):
            half[4 * i + p] = (both[p] * pres[p, i].astype(F32)).astype(BF16)
        return 0

    lax.fori_loop(0, 4, halve, 0)

    loads[6].wait()
    row = lax.broadcasted_iota(jnp.int32, (256, 256), 0)
    col = lax.broadcasted_iota(jnp.int32, (256, 256), 1)
    natural = ((row // 8) % 4) * 64 + ((row // 4) % 2) * 32 + ((row // 32) % 4) * 8 + (row // 128) * 4 + row % 4
    order = (col == natural).astype(BF16)

    def put(e, total):
        placed = jnp.dot(order, total.astype(BF16), preferred_element_type=F32).astype(BF16)
        part[e, 0] = placed[:128]
        part[e, 1] = placed[128:]

    def target_sum(e, _):
        total = jnp.zeros((256, 256), F32)
        for p in range(4):
            src = e - 1 - chg[p]
            inside = jnp.logical_and(src >= 0, src <= 3)
            clipped = jnp.clip(src, 0, 3)
            lhs = half[jnp.where(inside, 4 * clipped + p, 16)]
            total = total + lax.dot_general(lhs, right[4 * p + clipped], NT, preferred_element_type=F32)
        put(e, total)
        return 0

    outside = [jnp.zeros((256, 256), F32), jnp.zeros((256, 256), F32)]
    for p in range(4):
        low, high = chg[p] == -1, chg[p] == 1
        lhs = half[jnp.where(low, p, jnp.where(high, 12 + p, 16))]
        both = lax.dot_general(lhs, right[4 * p + jnp.where(low, 0, 3)], NT, preferred_element_type=F32)
        outside[0] = outside[0] + both * low.astype(F32)
        outside[1] = outside[1] + both * high.astype(F32)
    put(0, outside[0])
    put(5, outside[1])

    def to_core(g):
        some = pl.ds(3 * g, 3)
        return pltpu.make_async_remote_copy(
            part.at[some, 1 - c], c_in.at[some], c_s.at[g], c_r.at[g], device_id=(core_peer, s), device_id_type=MESH)

    def to_x(g, o):
        some = pl.ds(3 * g, 3)
        return pltpu.make_async_remote_copy(
            x_out.at[some, (x + o + 1) % 4], x_in.at[o, some], x_s.at[g, o], x_r.at[g, o],
            device_id=(x_peer[o], s), device_id_type=MESH)

    for g in (0, 1):
        lax.fori_loop(1 + 2 * g, 3 + 2 * g, target_sum, 0)
        to_core(g).start()

    for i in (0, 3):
        rotate(i)

    @pl.when(s > 0)
    def _():
        to_above().wait_recv()
        rot_t[0] = rot_in[0].T

    @pl.when(s < 3)
    def _():
        to_below().wait_recv()
        rot_t[5] = rot_in[1].T

    def outer(q, _):
        all_of(3 * q)
        return 0

    lax.fori_loop(0, 2, outer, 0)
    send_far((0, 3))
    send_across((0,))
    def core_sum(e, _):
        both = part[e, c].astype(F32) + c_in[e].astype(F32)
        x_out[e] = both.reshape(4, 32, 256).astype(BF16)
        return 0

    for g in (0, 1):
        to_core(g).wait_recv()
        lax.fori_loop(3 * g, 3 * g + 3, core_sum, 0)
        for o in range(3):
            to_x(g, o).start()
    hand_on([b for b in MIDDLE if b[0] in (1, 2)], hand_up, hand_down)
    send_beside((0, 3))
    send_ring((0, 1, 2, 3))
    for g in (0, 1):
        for o in range(3):
            to_x(g, o).wait_recv()
    rows = pl.ds(pl.multiple_of(x * 32, 32), 32)

    def x_sum(e, _):
        total = part[e, c, rows].astype(F32) + c_in[e, rows].astype(F32)
        for o in range(3):
            total = total + x_in[o, e].astype(F32)
        for q in range(4):
            f2[q, e] = total[8 * q:8 * q + 8]
        return 0

    lax.fori_loop(0, 6, x_sum, 0)
    for q in range(4):
        y_out[q] = f2[q].reshape(48, 256).astype(BF16)
    to_y = []
    for o in range(3):
        copy = pltpu.make_async_remote_copy(
            y_out.at[(y + o + 1) % 4], y_in.at[o], y_s.at[o], y_r.at[o],
            device_id=(y_peer[o], s), device_id_type=MESH)
        copy.start()
        to_y.append(copy)
    send_across((3,))
    hand_on(SIDE, side_up, side_down)
    hand_on([b for b in MIDDLE if b[0] in (0, 3)], hand_up, hand_down)
    for copy in to_y:
        copy.wait_recv()
    total = f2[y].reshape(48, 256)
    for o in range(3):
        total = total + y_in[o].astype(F32)
    z_out[...] = total[8:40].astype(BF16)
    e_out[0] = total[0:8]
    e_out[1] = total[40:48]
    to_z = pltpu.make_async_remote_copy(
        z_out, z_in, z_s.at[0], z_r.at[0], device_id=(zh_peer, s), device_id_type=MESH)
    to_z.start()

    def edge(side, far):
        op_to = zh_peer if far else d
        sec_to = s + 1 if side else s - 1
        return pltpu.make_async_remote_copy(
            e_out.at[side], e_in.at[side, far], e_s.at[side, far], e_r.at[side, far],
            device_id=(op_to, sec_to), device_id_type=MESH)

    @pl.when(s < 3)
    def _():
        edge(1, 0).start()
        edge(1, 1).start()

    @pl.when(s > 0)
    def _():
        edge(0, 0).start()
        edge(0, 1).start()

    to_z.wait_recv()
    mine = (total[8:40] + z_in[...].astype(F32)).reshape(4, 8, 256)
    f2[0, pl.ds(0, 4)] = mine

    @pl.when(s > 0)
    def _():
        edge(1, 0).wait_recv()
        edge(1, 1).wait_recv()
        f2[0, 0] = f2[0, 0] + e_in[1, 0] + e_in[1, 1]

    @pl.when(s < 3)
    def _():
        edge(0, 0).wait_recv()
        edge(0, 1).wait_recv()
        f2[0, 3] = f2[0, 3] + e_in[0, 0] + e_in[0, 1]

    final = f2[0, pl.ds(0, 4)] * (1.0 / 16.0)
    sig[...] = jnp.where(zh == 0, final[:, 0:4], final[:, 4:8])

    for copy in [to_z] + to_y:
        copy.wait_send()
    for g in (0, 1):
        to_core(g).wait_send()
        for o in range(3):
            to_x(g, o).wait_send()

    @pl.when(s < 3)
    def _():
        edge(1, 0).wait_send()
        edge(1, 1).wait_send()
        to_above().wait_send()

    @pl.when(s > 0)
    def _():
        edge(0, 0).wait_send()
        edge(0, 1).wait_send()
        to_below().wait_send()

    for k, here, blocks in (
        (1, hand_up, MIDDLE), (2, hand_down, MIDDLE), (1, side_up, SIDE), (2, side_down, SIDE),
    ):
        @pl.when(here)
        def _(k=k, blocks=blocks):
            for i, j in blocks:
                from_hand(k, j, i).wait_send()

    for k in (1, 2, 3):
        for j in (0, 1):
            for i in range(4):
                moved(k, j, i).wait()


def body(wavefunction, left_operators, right_operators, rotations, charges, present_blocks, directions):
    hbm = pl.BlockSpec(memory_space=pltpu.HBM)
    vmem = pl.BlockSpec(memory_space=pltpu.VMEM)
    smem = pl.BlockSpec(memory_space=pltpu.SMEM)
    dma = pltpu.SemaphoreType.DMA
    sigma, regrouped = pl.pallas_call(
        kernel,
        out_shape=(
            pltpu.VMEM((4, 4, 256), F32),
            pltpu.VMEM((8, 4, 256, 256), BF16),
        ),
        in_specs=[smem, smem, smem, hbm, hbm, hbm, hbm],
        out_specs=(vmem, vmem),
        scratch_shapes=[
            pltpu.VMEM((4, 256, 256), BF16),
            pltpu.VMEM((4, 4, 256, 256), BF16),
            pltpu.VMEM((16, 256, 256), BF16),
            pltpu.VMEM((4, 256, 256), BF16),
            pltpu.VMEM((6, 256, 256), BF16),
            pltpu.VMEM((2, 256, 256), BF16),
            pltpu.VMEM((17, 256, 256), BF16),
            pltpu.VMEM((16, 256, 256), BF16),
            pltpu.VMEM((6, 4, 256, 256), BF16),
            pltpu.VMEM((8, 256, 256), BF16),
            pltpu.VMEM((6, 2, 128, 256), BF16),
            pltpu.VMEM((6, 128, 256), BF16),
            pltpu.VMEM((6, 4, 32, 256), BF16),
            pltpu.VMEM((3, 6, 32, 256), BF16),
            pltpu.VMEM((4, 6, 8, 256), F32),
            pltpu.VMEM((4, 48, 256), BF16),
            pltpu.VMEM((3, 48, 256), BF16),
            pltpu.VMEM((32, 256), BF16),
            pltpu.VMEM((32, 256), BF16),
            pltpu.VMEM((2, 8, 256), F32),
            pltpu.VMEM((2, 2, 8, 256), F32),
            dma((7,)), dma((2,)), dma((2,)), dma((6, 4)), dma((6, 4)), dma((8,)), dma((8,)),
            dma((2,)), dma((2,)), dma((2, 3)), dma((2, 3)), dma((3,)), dma((3,)),
            dma((1,)), dma((1,)), dma((2, 2)), dma((2, 2)),
        ],
        compiler_params=pltpu.CompilerParams(
            collective_id=0, has_side_effects=True, vmem_limit_bytes=58000000),
        name="step",
    )(
        charges, present_blocks, directions.reshape(4),
        wavefunction,
        left_operators,
        right_operators.reshape(16, 256, 256),
        rotations,
    )
    return sigma, regrouped


def solution(mesh):
    placed = (
        P("sec", None, None),
        P("op", "sec", None, None),
        P("op", "sec", None, None),
        P("sec", None, None),
        P("op"),
        P("op", "sec"),
        P("op", None),
    )
    return jax.shard_map(
        body,
        mesh=mesh,
        in_specs=placed,
        out_specs=(P("sec", "op", None), P("op", "sec", None, None)),
        check_vma=False,
    )
```
